256 devices in a mesh: beam: 8 (over x, core), row: 32 (over y, z).
Axes of the slice: x: 4, y: 4, z: 8, core: 2. Of those that a mesh axis runs over, the one named last changes fastest.
Arguments:
- x_in: bfloat16 [4, 2, 16, 8192], P(None, None, None, 'beam'), may hold values from -6 to 6
- w_inner: bfloat16 [8192, 2, 16384], P('beam', None, 'row'), may hold values from -0.0625 to 0.0625
- w_bc: bfloat16 [8192, 2, 2048], P('beam', None, 'row'), may hold values from -0.0625 to 0.0625
- w_dt: bfloat16 [8192, 256], P('beam', 'row'), may hold values from -0.0625 to 0.0625
- conv_x_w: bfloat16 [4, 16384], P(None, 'row'), may hold values from -3 to 3
- conv_bc_w: bfloat16 [4, 2, 2048], P(None, None, 'row'), may hold values from -3 to 3
- dt_bias: float32 [256], P('row'), may hold values from -4 to 1
- a_log: float32 [256], P('row'), may hold values from 0 to 2.8
- d_skip: float32 [256], P('row'), may hold values from 0.5 to 2
- norm_gain: float32 [16384], P('row'), may hold values from 0.1 to 1.9
- w_out: bfloat16 [16384, 8192], P('row', 'beam'), may hold values from -0.046875 to 0.046875
- ssm_state: bfloat16 [2, 16, 256, 64, 256], P(None, 'beam', 'row'), may hold values from -6 to 6
- conv_x_state: bfloat16 [2, 16, 256, 64, 3], P(None, 'beam', 'row'), may hold values from -6 to 6
- conv_bc_state: bfloat16 [2, 16, 3, 2, 2048], P(None, 'beam', None, None, 'row'), may hold values from -6 to 6
- parents: int32 [4, 2, 16], replicated, may hold values from 0 to 15
Outputs:
- layer_out: bfloat16 [4, 32, 8192], P(None, 'row', 'beam')
- ssm_final: bfloat16 [2, 16, 256, 64, 256], P(None, 'beam', 'row')
- conv_x_final: bfloat16 [2, 16, 256, 64, 3], P(None, 'beam', 'row')
- conv_bc_final: bfloat16 [2, 16, 3, 2, 2048], P(None, 'beam', None, None, 'row')
The draws below stay inside these ranges and needn't reach their ends.
All inputs are finite; a program needn't handle non-finite values.
Results may differ from the reference program's by a relative error of at most 0.0077.
Values may be sent and summed in bfloat16 or wider, within the bound.
No kernel may reach another device: no remote copies, remote signals or barrier semaphores. Data moves between devices by JAX's collectives and lax.ppermute only.
A program may use at most 64 MiB of HBM per device.

```python
import jax
import jax.numpy as jnp
from jax import lax

D = 8192
HEADS = 256
HDIM = 64
NSTATE = 256
GROUPS = 8
CONV = 4
BEAM_WIDTH = 16
SESS = 2
STEPS = 4
INNER = 16384
GN = 2048
BEAMS = 32


def plant(values, key, smallest, top_value):
    longest = values.shape.index(max(values.shape))
    spots = []
    for shift in (0, 1):
        where = [jax.random.randint(jax.random.fold_in(key, axis), (), 0, length) for axis, length in enumerate(values.shape)]
        where[longest] = (where[longest] + shift) % values.shape[longest]
        spots.append(tuple(where))
    return values.at[spots[0]].set(smallest).at[spots[1]].set(top_value)


def level_of(rng, extent, shards, smallest, top_value):
    level, own = 1.0, jax.random.fold_in(rng, 6)
    for axis_at, parts in shards:
        draws = jnp.exp(jax.random.uniform(jax.random.fold_in(own, axis_at), (parts,), jnp.float32, smallest / len(shards), top_value / len(shards)))
        level = level * jnp.repeat(draws, extent[axis_at] // parts).reshape([-1 if axis == axis_at else 1 for axis in range(len(extent))])
    return level


def noise(key, extent, scale, limit, pieces=(), dtype=jnp.bfloat16):
    values = jax.random.normal(key, extent, jnp.float32) * scale
    if len(pieces) > 0:
        values = level_of(key, extent, pieces, -0.22, 0.18) * values
    return jnp.clip(values, min=-limit, max=limit).astype(dtype)


def setup_inputs(seed: int = 0) -> dict:
    key_list = jax.random.split(jax.random.key(seed), 16)
    return {
        "x_in": noise(key_list[0], (STEPS, SESS, BEAM_WIDTH, D), 1.0, 6.0, ((3, 8),)),
        "w_inner": noise(key_list[1], (D, 2, INNER), D ** -0.5, 0.0625, ((0, 8), (2, 32))),
        "w_bc": noise(key_list[2], (D, 2, GN), D ** -0.5, 0.0625, ((0, 8), (2, 32))),
        "w_dt": noise(key_list[3], (D, HEADS), D ** -0.5, 0.0625, ((0, 8), (1, 32))),
        "conv_x_w": noise(key_list[4], (CONV, INNER), CONV ** -0.5, 3.0, ((1, 32),)),
        "conv_bc_w": noise(key_list[5], (CONV, 2, GN), CONV ** -0.5, 3.0, ((2, 32),)),
        "dt_bias": jnp.clip(-4.0 + 5.0 * jax.random.uniform(key_list[6], (HEADS,), jnp.float32) ** level_of(key_list[6], (HEADS,), ((0, 32),), -0.2, 0.2), -4.0, 1.0),
        "a_log": jnp.clip(2.8 * jax.random.uniform(key_list[7], (HEADS,), jnp.float32) ** level_of(key_list[7], (HEADS,), ((0, 32),), -0.2, 0.2), 0.0, 2.8),
        "d_skip": jnp.clip(0.5 + 1.5 * jax.random.uniform(key_list[8], (HEADS,), jnp.float32) ** level_of(key_list[8], (HEADS,), ((0, 32),), -0.2, 0.2), 0.5, 2.0),
        "norm_gain": jnp.clip(1.0 + 0.18 * jax.random.normal(key_list[9], (INNER,), jnp.float32), 0.1, 1.9),
        "w_out": noise(key_list[10], (INNER, D), INNER ** -0.5, 0.046875, ((0, 32), (1, 8))),
        "ssm_state": noise(key_list[11], (SESS, BEAM_WIDTH, HEADS, HDIM, NSTATE), 1.0, 6.0, ((1, 8), (2, 32))),
        "conv_x_state": noise(key_list[12], (SESS, BEAM_WIDTH, HEADS, HDIM, CONV - 1), 1.0, 6.0, ((1, 8), (2, 32))),
        "conv_bc_state": noise(key_list[13], (SESS, BEAM_WIDTH, CONV - 1, 2, GN), 1.0, 6.0, ((1, 8), (4, 32))),
        "parents": plant(jax.random.randint(key_list[14], (STEPS, SESS, BEAM_WIDTH), 0, BEAM_WIDTH), jax.random.fold_in(key_list[14], 1), 0, BEAM_WIDTH - 1).astype(jnp.int32),
    }


EPS = 1e-05

def stored(value):
    return lax.optimization_barrier(value.astype(jnp.bfloat16))

def reference(x_in, w_inner, w_bc, w_dt, conv_x_w, conv_bc_w, dt_bias, a_log, d_skip, norm_gain, w_out, ssm_state, conv_x_state, conv_bc_state, parents):
    group_heads = HEADS // GROUPS
    ssm_held = ssm_state
    conv_held = conv_x_state
    rim_held = conv_bc_state
    conv_taps = conv_x_w.astype(jnp.float32).reshape(CONV, HEADS, HDIM)
    bc_taps = conv_bc_w.astype(jnp.float32)
    decay_rates = jnp.exp(a_log.astype(jnp.float32))
    gains = norm_gain.astype(jnp.float32).reshape(HEADS, HDIM)
    picker = jax.vmap(lambda held, chosen: held[chosen])
    outputs = []
    for step in range(STEPS):
        parent = parents[step]
        ssm_held = picker(ssm_held, parent)
        conv_held = picker(conv_held, parent)
        rim_held = picker(rim_held, parent)
        tokens = x_in[step].reshape(BEAMS, D)
        inner = stored(jnp.dot(tokens, w_inner.reshape(D, 2 * INNER), preferred_element_type=jnp.float32))
        inner = inner.reshape(SESS, BEAM_WIDTH, 2, HEADS, HDIM)
        gate_in = inner[:, :, 0]
        x_new = inner[:, :, 1]
        bc_new = stored(jnp.dot(tokens, w_bc.reshape(D, 2 * GN), preferred_element_type=jnp.float32))
        bc_new = bc_new.reshape(SESS, BEAM_WIDTH, 2, GN)
        dt_raw = stored(jnp.dot(tokens, w_dt, preferred_element_type=jnp.float32)).reshape(SESS, BEAM_WIDTH, HEADS)
        mixed = lax.optimization_barrier(jnp.sum(conv_held.astype(jnp.float32) * jnp.transpose(conv_taps[:-1], (1, 2, 0)), axis=-1))
        mixed = mixed + conv_taps[-1] * x_new.astype(jnp.float32)
        x_conv = stored(jax.nn.silu(mixed))
        conv_held = jnp.concatenate([conv_held[..., 1:], x_new[..., None]], axis=-1)
        mixed_bc = lax.optimization_barrier(jnp.sum(rim_held.astype(jnp.float32) * bc_taps[:-1], axis=2)) + bc_taps[-1] * bc_new.astype(jnp.float32)
        bc_conv = stored(jax.nn.silu(mixed_bc))
        rim_held = jnp.concatenate([rim_held[:, :, 1:], bc_new[:, :, None]], axis=2)
        b_in = jnp.repeat(bc_conv[:, :, 0].reshape(SESS, BEAM_WIDTH, GROUPS, NSTATE), group_heads, axis=2).astype(jnp.float32)
        c_out = jnp.repeat(bc_conv[:, :, 1].reshape(SESS, BEAM_WIDTH, GROUPS, NSTATE), group_heads, axis=2).astype(jnp.float32)
        step_size = jax.nn.softplus(dt_raw.astype(jnp.float32) + dt_bias.astype(jnp.float32))
        decay = jnp.exp(-decay_rates * step_size)
        x_val = x_conv.astype(jnp.float32)
        state = decay[..., None, None] * ssm_held.astype(jnp.float32) + (step_size[..., None] * x_val)[..., None] * b_in[:, :, :, None, :]
        read = lax.optimization_barrier(jnp.sum(state * c_out[:, :, :, None, :], axis=-1)) + d_skip.astype(jnp.float32)[:, None] * x_val
        ssm_held = stored(state)
        gated = read * jax.nn.silu(gate_in.astype(jnp.float32))
        grouped = gated.reshape(SESS, BEAM_WIDTH, GROUPS, group_heads * HDIM)
        mean_sq = lax.optimization_barrier(jnp.sum(grouped * grouped, axis=-1, keepdims=True)) / (group_heads * HDIM)
        scaled = (grouped * lax.rsqrt(mean_sq + EPS)).reshape(SESS, BEAM_WIDTH, HEADS, HDIM)
        normed = stored(scaled * gains)
        result = jnp.dot(normed.reshape(BEAMS, INNER), w_out, preferred_element_type=jnp.float32).astype(jnp.bfloat16)
        outputs.append(result)
    return (jnp.stack(outputs), ssm_held, conv_held, rim_held)
```

```python
import jax
import jax.numpy as jnp
from jax import lax
from jax.experimental import pallas as pl
from jax.experimental.pallas import tpu as pltpu
from jax.sharding import PartitionSpec as P

EPS = 1e-05
F32 = jnp.float32
BF16 = jnp.bfloat16
STEPS = 4
SESS = 2
WIDTH = 16
BEAMS = SESS * WIDTH
ROWS = STEPS * BEAMS
HD = 64
NS = 256
GROUP_CH = 2048.0


def row_of(step, s, b):
    v = s * WIDTH + b
    return (v % 4) * 32 + (v // 4) * 4 + step


def dot(a, b):
    return jnp.dot(a, b, preferred_element_type=F32)


def dot_t(a, b):
    return lax.dot_general(a, b, (((1,), (1,)), ((), ())), preferred_element_type=F32)


def lineage(par):
    r = lax.broadcasted_iota(jnp.int32, (ROWS, 1), 0)
    t = r & 3
    s = (r & 31) >> 4
    before = (par & 3) * 32 + (s * 4 + (par >> 2)) * 4 + t - 1
    before = jnp.where(t > 0, before, -1)
    start = jnp.where(t == 0, (par >> 1) * 4 + s * 2 + (par & 1), -1)
    lanes = lax.broadcasted_iota(jnp.int32, (ROWS, ROWS), 1)
    a1 = jnp.where(lanes == before, 1.0, 0.0)
    lanes_i = lax.broadcasted_iota(jnp.int32, (ROWS, BEAMS), 1)
    g = jnp.where(lanes_i == start, 1.0, 0.0)
    a1b = a1.astype(BF16)
    a2 = dot(a1b, a1b)
    a3 = dot(a1b, a2.astype(BF16))
    gb = g.astype(BF16)
    g1 = dot(a1b, gb)
    g2 = dot(a1b, g1.astype(BF16))
    g3 = dot(a1b, g2.astype(BF16))
    return t, a1, a2, a3, g + g1 + g2 + g3


def conv_kernel(recv, par, taps, sum_out, conv_out, bc_out, dt_out, fin_out, init):
    total = recv[0, 0:ROWS, :].astype(F32)
    dt = recv[0, 128:144, :].astype(F32)
    for k in range(3):
        init[k, 0:4, :] = dt[4 * k : 4 * k + 4]
    for i in range(1, 8):
        total = total + recv[i, 0:ROWS, :].astype(F32)
        extra = recv[i, 128:144, :].astype(F32)
        for k in range(3):
            init[k, 4 * i : 4 * i + 4, :] = extra[4 * k : 4 * k + 4]
        dt = dt + extra
    dt_out[...] = dt[12:13, 0:128] + dt[12:13, 128:256]
    new = total.astype(BF16)
    t, a1, a2, a3, g = lineage(par[...])
    gb = g.astype(BF16)
    start = [dot(gb, init[k].astype(BF16)) for k in range(3)]
    past1 = dot(a1.astype(BF16), new) + jnp.where(t == 0, start[2], 0.0)
    past2 = dot(a2.astype(BF16), new) + jnp.where(t == 0, start[1], 0.0) + jnp.where(t == 1, start[2], 0.0)
    past3 = (
        dot(a3.astype(BF16), new)
        + jnp.where(t == 0, start[0], 0.0)
        + jnp.where(t == 1, start[1], 0.0)
        + jnp.where(t == 2, start[2], 0.0)
    )
    w = taps[...]
    mixed = w[0:1] * past3 + w[1:2] * past2 + w[2:3] * past1 + w[3:4] * new.astype(F32)
    conv = mixed / (1.0 + jnp.exp(-mixed))
    sum_out[...] = new
    conv_out[...] = conv[:, 0:128].astype(BF16)
    bc_out[...] = conv[:, 128:256].astype(BF16)
    e = lax.broadcasted_iota(jnp.int32, (BEAMS, ROWS), 0)
    b = (e >> 2) * 2 + (e & 1)
    s = (e >> 1) & 1
    last = (b & 3) * 32 + (s * 4 + (b >> 2)) * 4 + STEPS - 1
    pick = jnp.where(lax.broadcasted_iota(jnp.int32, (BEAMS, ROWS), 1) == last, 1.0, 0.0).astype(BF16)
    fin_out[0] = dot(pick, past2.astype(BF16)).astype(BF16)
    fin_out[1] = dot(pick, past1.astype(BF16)).astype(BF16)
    fin_out[2] = dot(pick, new).astype(BF16)


def group_columns(blocks, low_row):
    b_cols, c_cols = [], []
    for q in range(4):
        part = jnp.zeros((ROWS, 128), F32)
        for k in range(4):
            part = part + jnp.where(low_row == float(q ^ k), blocks[k], 0.0)
        b_cols.append(part[:, 0:64])
        c_cols.append(part[:, 64:128])
    return jnp.concatenate(b_cols, 1).astype(BF16), jnp.concatenate(c_cols, 1).astype(BF16)


def scan_kernel(
    par, new, conv, bc0, bc1, bc2, bc3, dt_raw, consts, state, send_out, b_out, coef_out, first_out
):
    blocks = [ref[...].astype(F32) for ref in (bc0, bc1, bc2, bc3)]
    b_in, c_out = group_columns(blocks, consts[4:5])
    t, a1, a2, a3, g = lineage(par[...])
    raw = dt_raw[...].astype(BF16).astype(F32) + consts[2:3]
    step_size = jnp.maximum(raw, 0.0) + jnp.log1p(jnp.exp(-jnp.abs(raw)))
    rate = jnp.exp(consts[1:2])
    log_decay = -rate * step_size
    rr = lax.broadcasted_iota(jnp.int32, (ROWS, ROWS), 0)
    cc = lax.broadcasted_iota(jnp.int32, (ROWS, ROWS), 1)
    eye = jnp.where(rr == cc, 1.0, 0.0)
    path1 = jnp.sum(eye * log_decay, axis=1, keepdims=True)
    path2 = path1 + jnp.sum(a1 * log_decay, axis=1, keepdims=True)
    path3 = path2 + jnp.sum(a2 * log_decay, axis=1, keepdims=True)
    path4 = path3 + jnp.sum(a3 * log_decay, axis=1, keepdims=True)
    coef = (eye + a1 * jnp.exp(path1) + a2 * jnp.exp(path2) + a3 * jnp.exp(path3)) * step_size
    first = jnp.exp(path4)
    x_conv = conv[:, 0:64]
    inner = dot_t(c_out, b_in) * coef
    read = jnp.dot(inner, x_conv.astype(F32), precision=lax.Precision.HIGHEST, preferred_element_type=F32)
    lanes_i = lax.broadcasted_iota(jnp.int32, (ROWS, BEAMS), 1).astype(F32)
    origin = jnp.sum(g * lanes_i, axis=1, keepdims=True)
    half = jnp.where(lax.broadcasted_iota(jnp.int32, (ROWS, 128), 1) < 64, 0.0, 1.0)
    origin_b = jnp.broadcast_to(origin, (ROWS, 128)) - half
    acc = jnp.zeros((ROWS, 128), F32)
    for p in range(BEAMS // 2):
        both = state[2 * p : 2 * p + 2].reshape(2 * HD, NS)
        acc = acc + jnp.where(origin_b == float(2 * p), dot_t(c_out, both), 0.0)
    old = acc[:, 0:64] + acc[:, 64:128]
    x_val = x_conv.astype(F32)
    read = read + first * old + consts[3:4, 0:64] * x_val
    gate = new[:, 64:128].astype(F32)
    gated = read * (gate / (1.0 + jnp.exp(-gate)))
    square = jnp.sum(gated * gated, axis=1, keepdims=True)
    high = square.astype(BF16).astype(F32)
    rest = square - high
    lane = lax.broadcasted_iota(jnp.int32, (ROWS, 64), 1)
    stats = jnp.where(lane == 0, high, jnp.where(lane == 1, rest, 0.0))
    send_out[...] = jnp.concatenate([gated * consts[0:1, 0:64], stats], axis=1).astype(BF16)
    b_out[...] = b_in
    coef_out[...] = coef
    first_out[...] = jnp.broadcast_to(first, (ROWS, 128))


def final_kernel(parents, conv, b_in, coef, first, state, fin, out):
    x_t = conv[:, 0:128].astype(F32).T[0:64]
    b = b_in[...]
    for i in range(8):
        for j in range(4):
            s, beam = j // 2, 2 * i + j % 2
            row = row_of(STEPS - 1, s, beam)
            at = beam
            for step in range(STEPS - 1, -1, -1):
                at = parents[step * BEAMS + s * WIDTH + at]
            origin = (at >> 1) * 4 + s * 2 + (at & 1)
            left = (x_t * coef[row : row + 1, :]).astype(BF16)
            update = dot(left, b)
            keep = jnp.broadcast_to(first[row : row + 1, 0:1], (HD, NS))
            out[i, HD * j : HD * j + HD, :] = (keep * state[origin].astype(F32) + update).astype(BF16)
        taps = [fin[k, 4 * i : 4 * i + 4, 0:64].astype(F32) for k in range(3)]
        block = jnp.concatenate(taps + [jnp.zeros((4, 64), F32)], axis=1)
        out[i, 4 * HD : 4 * HD + 16, :] = jnp.concatenate([block, jnp.zeros((12, NS), F32)], axis=0).astype(BF16)


def out_kernel(place, recv, w_out, o0, o1, o2, o3, acc):
    low = place[1]
    stats = recv[0, :, 64:128].astype(F32)
    for i in range(1, 8):
        stats = stats + recv[i, :, 64:128].astype(F32)
    square = stats[:, 0:1] + stats[:, 1:2]
    high = square.astype(BF16).astype(F32)
    rest = square - high
    lane = lax.broadcasted_iota(jnp.int32, (ROWS, 128), 1)
    acc[:, 1024:1152] = jnp.where(lane == 0, high, jnp.where(lane == 1, rest, 0.0))
    left = jnp.concatenate([recv[i, :, 0:64] for i in range(8)], axis=1)
    acc[:, 0:1024] = dot(left, w_out[...])
    for k, ref in enumerate((o0, o1, o2, o3)):
        ref[...] = acc[pl.ds(pl.multiple_of((low ^ k) * 32, 32), 32), :].astype(BF16)


def norm_kernel(place, p0, p1, p2, p3, *refs):
    outs, acc = refs[:8], refs[8]
    total = p0[...].astype(F32) + p1[...].astype(F32) + p2[...].astype(F32) + p3[...].astype(F32)
    square = total[:, 1024:1025] + total[:, 1025:1026]
    scale = lax.rsqrt(square * (1.0 / GROUP_CH) + EPS)
    normed = total[:, 0:1024] * scale
    for m in range(8):
        acc[m] = normed[STEPS * m : STEPS * m + STEPS]
    for k, ref in enumerate(outs):
        ref[...] = acc[place[0] ^ k].astype(BF16)


def sum_kernel(p0, p1, p2, p3, p4, p5, p6, p7, out):
    total = p0[...].astype(F32)
    for ref in (p1, p2, p3, p4, p5, p6, p7):
        total = total + ref[...].astype(F32)
    out[...] = total.astype(BF16)


VM = pl.BlockSpec(memory_space=pltpu.VMEM)
SM = pl.BlockSpec(memory_space=pltpu.SMEM)
FAR = pl.BlockSpec(memory_space=pltpu.HBM)


def call(kernel, name, specs, outs, scratch=(), mib=6):
    def build(*args):
        far = [n for n, spec in enumerate(specs) if spec is FAR]
        count = len(specs)
        buffers = [pltpu.VMEM(args[n].shape, args[n].dtype) for n in far]
        sems = [pltpu.SemaphoreType.DMA((len(far),))] if far else []

        def body(*refs):
            ins = list(refs[:count])
            rest = refs[count : count + len(outs) + len(scratch)]
            held = refs[count + len(outs) + len(scratch) :]
            copies = [pltpu.make_async_copy(ins[n], held[k], held[-1].at[k]) for k, n in enumerate(far)]
            for copy in copies:
                copy.start()
            for copy in copies:
                copy.wait()
            for k, n in enumerate(far):
                ins[n] = held[k]
            kernel(*ins, *rest)

        return pl.pallas_call(
            body,
            name=name,
            in_specs=list(specs),
            out_specs=tuple(VM for _ in outs),
            out_shape=tuple(jax.ShapeDtypeStruct(s, d) for s, d in outs),
            scratch_shapes=list(scratch) + buffers + sems,
            compiler_params=pltpu.CompilerParams(vmem_limit_bytes=mib << 20),
        )(*args)

    return build


def swap(value, axis, count, mask):
    return lax.ppermute(value, axis, [(i, i ^ mask) for i in range(count)])


def local(
    x_in,
    w_inner,
    w_bc,
    w_dt,
    conv_x_w,
    conv_bc_w,
    dt_bias,
    a_log,
    d_skip,
    norm_gain,
    w_out,
    ssm_state,
    conv_x_state,
    conv_bc_state,
    parents,
):
    beam = lax.axis_index("beam")
    row = lax.axis_index("row")
    place = jnp.stack([beam, row & 3]).astype(jnp.int32)
    d_local = x_in.shape[-1]
    heads = ssm_state.shape[2]
    parent_column = parents.reshape(STEPS, 8, 4).transpose(2, 1, 0).reshape(ROWS, 1)
    x = x_in.reshape(STEPS, 8, 4, d_local).transpose(2, 1, 0, 3).reshape(ROWS, d_local)

    inner = jnp.einsum("rd,dzk->rzk", x, w_inner, preferred_element_type=F32).astype(BF16)
    inner = inner[:, ::-1].reshape(ROWS, 2, heads, HD).transpose(2, 0, 1, 3).reshape(heads, ROWS, 2 * HD)
    bc = jnp.einsum("rd,dzk->rzk", x, w_bc, preferred_element_type=F32).astype(BF16).reshape(ROWS, 128)
    top = jnp.concatenate([inner, jnp.broadcast_to(bc[None], (heads, ROWS, 128))], axis=2)
    dt = jnp.einsum("dh,rd->hr", w_dt, x, preferred_element_type=F32)
    dt_high = lax.reduce_precision(dt, 8, 7)
    dt_row = jnp.concatenate([dt_high, dt - dt_high], axis=1).astype(BF16)[:, None]
    taps_x = conv_x_state.transpose(2, 4, 0, 1, 3).reshape(heads, 12, HD)
    taps_bc = jnp.broadcast_to(conv_bc_state.transpose(2, 0, 1, 3, 4).reshape(1, 12, 128), (heads, 12, 128))
    extra = jnp.concatenate([taps_x, jnp.zeros((heads, 12, HD), BF16), taps_bc], axis=2)
    bottom = jnp.concatenate([extra, dt_row, jnp.zeros((heads, 3, 256), BF16)], axis=1)
    payload = jnp.concatenate([top, bottom], axis=1)
    recv = lax.all_to_all(payload, "beam", split_axis=0, concat_axis=0, tiled=True)

    conv_head = lax.dynamic_slice_in_dim(conv_x_w, beam * HD, HD, 1)
    taps = jnp.concatenate([conv_head, jnp.zeros((4, HD), BF16), conv_bc_w.reshape(4, 128)], axis=1).astype(F32)
    gain = jnp.pad(lax.dynamic_slice_in_dim(norm_gain, beam * HD, HD, 0), (0, HD)).reshape(1, 128)
    scalars = [lax.dynamic_slice_in_dim(v, beam, 1, 0) for v in (a_log, dt_bias, d_skip)] + [(row & 3).astype(F32)[None]]
    fills = [jnp.broadcast_to(v[:, None], (1, 128)) for v in scalars]
    consts = jnp.concatenate([gain] + fills + [jnp.zeros((3, 128), F32)], axis=0)
    by_head = ssm_state.transpose(2, 0, 1, 3, 4).reshape(heads, 4, HD, NS)
    taps, consts, by_head, place, parent_column = lax.optimization_barrier((taps, consts, by_head, place, parent_column))
    taps, consts, by_head, place, parent_column, recv = lax.optimization_barrier(
        (taps, consts, by_head, place, parent_column, recv)
    )
    state = lax.all_to_all(by_head, "beam", split_axis=0, concat_axis=0, tiled=True).reshape(BEAMS, HD, NS)

    new, conv, bc_conv, dt_raw, fin = call(
        conv_kernel,
        "conv",
        [FAR, VM, VM],
        [((ROWS, 256), BF16), ((ROWS, 128), BF16), ((ROWS, 128), BF16), ((1, ROWS), F32), ((3, BEAMS, 256), BF16)],
        [pltpu.VMEM((3, BEAMS, 256), F32)],
    )(recv, parent_column, taps)

    others = [swap(bc_conv, "row", 32, k) for k in (1, 2, 3)]

    send, b_in, coef, first = call(
        scan_kernel,
        "scan",
        [FAR] * 10,
        [((ROWS, 128), BF16), ((ROWS, NS), BF16), ((ROWS, ROWS), F32), ((ROWS, 128), F32)],
    )(parent_column, new, conv, bc_conv, *others, dt_raw, consts, state)

    gathered = lax.all_to_all(
        jnp.broadcast_to(send[None], (heads, ROWS, 128)), "beam", split_axis=0, concat_axis=0, tiled=True
    )
    (final,) = call(
        final_kernel,
        "final",
        [SM] + [FAR] * 6,
        [((heads, 4 * HD + 16, NS), BF16)],
    )(parents.reshape(ROWS), conv, b_in, coef, first, state, fin)
    home = lax.all_to_all(final, "beam", split_axis=0, concat_axis=0, tiled=True)

    parts = call(
        out_kernel,
        "project",
        [SM, FAR, VM],
        [((32, 1152), BF16)] * 4,
        [pltpu.VMEM((ROWS, 1152), F32)],
    )(place, gathered, w_out)
    got = [parts[0]] + [swap(parts[k], "row", 32, k) for k in (1, 2, 3)]
    place_z = jnp.stack([row >> 2]).astype(jnp.int32)
    pieces = call(norm_kernel, "norm", [SM] + [VM] * 4, [((STEPS, 1024), BF16)] * 8, [pltpu.VMEM((8, STEPS, 1024), F32)])(
        place_z, *got
    )
    far_first = (5, 7, 3, 1, 4, 6, 2)
    arrived = [pieces[0]] + [swap(pieces[k], "row", 32, k * 4) for k in far_first]
    (layer_out,) = call(sum_kernel, "total", [VM] * 8, [((STEPS, 1024), BF16)])(*arrived)
    layer_out = layer_out[:, None]

    ssm_final = home[:, : 4 * HD].reshape(heads, SESS, 2, HD, NS).transpose(1, 2, 0, 3, 4)
    conv_x_final = home[:, 4 * HD : 4 * HD + 4, :192].reshape(heads, SESS, 2, 3, HD).transpose(1, 2, 0, 4, 3)
    own = lax.dynamic_slice_in_dim(fin, beam * 4, 4, 1)[:, :, 128:]
    conv_bc_final = own.reshape(3, SESS, 2, 2, 64).transpose(1, 2, 0, 3, 4)
    return layer_out, ssm_final, conv_x_final, conv_bc_final


def solution(mesh):
    placed = (
        P(None, None, None, "beam"),
        P("beam", None, "row"),
        P("beam", None, "row"),
        P("beam", "row"),
        P(None, "row"),
        P(None, None, "row"),
        P("row"),
        P("row"),
        P("row"),
        P("row"),
        P("row", "beam"),
        P(None, "beam", "row", None, None),
        P(None, "beam", "row", None, None),
        P(None, "beam", None, None, "row"),
        P(),
    )
    return jax.shard_map(
        local,
        mesh=mesh,
        in_specs=placed,
        out_specs=(
            P(None, "row", "beam"),
            P(None, "beam", "row", None, None),
            P(None, "beam", "row", None, None),
            P(None, "beam", None, None, "row"),
        ),
        check_vma=False,
    )
```

```python
import jax
import jax.numpy as jnp
from jax import lax
from jax.experimental import pallas as pl
from jax.experimental.pallas import tpu as pltpu
from jax.sharding import PartitionSpec as P

EPS = 1e-05
F32 = jnp.float32
BF16 = jnp.bfloat16
STEPS = 4
SESS = 2
WIDTH = 16
BEAMS = SESS * WIDTH
ROWS = STEPS * BEAMS
HD = 64
NS = 256
GROUP_CH = 2048.0


def row_of(step, s, b):
    v = s * WIDTH + b
    return (v % 4) * 32 + (v // 4) * 4 + step


def dot(a, b):
    return jnp.dot(a, b, preferred_element_type=F32)


def dot_t(a, b):
    return lax.dot_general(a, b, (((1,), (1,)), ((), ())), preferred_element_type=F32)


def lineage(par):
    r = lax.broadcasted_iota(jnp.int32, (ROWS, 1), 0)
    t = r & 3
    s = (r & 31) >> 4
    before = (par & 3) * 32 + (s * 4 + (par >> 2)) * 4 + t - 1
    before = jnp.where(t > 0, before, -1)
    start = jnp.where(t == 0, (par >> 1) * 4 + s * 2 + (par & 1), -1)
    lanes = lax.broadcasted_iota(jnp.int32, (ROWS, ROWS), 1)
    a1 = jnp.where(lanes == before, 1.0, 0.0)
    lanes_i = lax.broadcasted_iota(jnp.int32, (ROWS, BEAMS), 1)
    g = jnp.where(lanes_i == start, 1.0, 0.0)
    a1b = a1.astype(BF16)
    a2 = dot(a1b, a1b)
    a3 = dot(a1b, a2.astype(BF16))
    gb = g.astype(BF16)
    g1 = dot(a1b, gb)
    g2 = dot(a1b, g1.astype(BF16))
    g3 = dot(a1b, g2.astype(BF16))
    return t, a1, a2, a3, g + g1 + g2 + g3


def head_part(ref, width):
    head = lax.axis_index("beam")
    part = jnp.zeros((ref.shape[0], width), F32)
    for h in range(8):
        part = part + jnp.where(head == h, ref[:, width * h : width * h + width].astype(F32), 0.0)
    return part


def head_value(ref):
    lane = lax.broadcasted_iota(jnp.int32, (1, 8), 1)
    return jnp.sum(jnp.where(lane == lax.axis_index("beam"), ref[...], 0.0), axis=1, keepdims=True)


def pack_kernel(state, *refs):
    outs, (held, sem_in, sem_out) = refs[:8], refs[8:]
    head = lax.axis_index("beam")
    loads = []
    for k in range(8):
        for j in range(4):
            loads.append(pltpu.make_async_copy(state.at[j // 2, j % 2, head ^ k], held.at[k, j], sem_in.at[k, j]))
            loads[-1].start()
    copies = []
    for k in range(8):
        for j in range(4):
            loads[4 * k + j].wait()
        copies.append(pltpu.make_async_copy(held.at[k], outs[k], sem_out.at[k]))
        copies[-1].start()
    for copy in copies:
        copy.wait()


def conv_kernel(recv, par, conv_x_w, conv_bc_w, sum_out, conv_out, bc_out, dt_out, fin_out, init):
    total = recv[0, 0:ROWS, :].astype(F32)
    dt = recv[0, 128:144, :].astype(F32)
    for k in range(3):
        init[k, 0:4, :] = dt[4 * k : 4 * k + 4]
    for i in range(1, 8):
        total = total + recv[i, 0:ROWS, :].astype(F32)
        extra = recv[i, 128:144, :].astype(F32)
        for k in range(3):
            init[k, 4 * i : 4 * i + 4, :] = extra[4 * k : 4 * k + 4]
        dt = dt + extra
    dt_out[...] = dt[12:13, 0:128] + dt[12:13, 128:256]
    new = total.astype(BF16)
    t, a1, a2, a3, g = lineage(par[...])
    gb = g.astype(BF16)
    start = [dot(gb, init[k].astype(BF16)) for k in range(3)]
    past1 = dot(a1.astype(BF16), new) + jnp.where(t == 0, start[2], 0.0)
    past2 = dot(a2.astype(BF16), new) + jnp.where(t == 0, start[1], 0.0) + jnp.where(t == 1, start[2], 0.0)
    past3 = (
        dot(a3.astype(BF16), new)
        + jnp.where(t == 0, start[0], 0.0)
        + jnp.where(t == 1, start[1], 0.0)
        + jnp.where(t == 2, start[2], 0.0)
    )
    w = jnp.concatenate([head_part(conv_x_w, HD), jnp.zeros((4, HD), F32), conv_bc_w[...].astype(F32)], axis=1)
    mixed = w[0:1] * past3 + w[1:2] * past2 + w[2:3] * past1 + w[3:4] * new.astype(F32)
    conv = mixed / (1.0 + jnp.exp(-mixed))
    sum_out[...] = new
    conv_out[...] = conv[:, 0:128].astype(BF16)
    bc_out[...] = conv[:, 128:256].astype(BF16)
    e = lax.broadcasted_iota(jnp.int32, (BEAMS, ROWS), 0)
    b = (e >> 2) * 2 + (e & 1)
    s = (e >> 1) & 1
    last = (b & 3) * 32 + (s * 4 + (b >> 2)) * 4 + STEPS - 1
    pick = jnp.where(lax.broadcasted_iota(jnp.int32, (BEAMS, ROWS), 1) == last, 1.0, 0.0).astype(BF16)
    fin_out[0] = dot(pick, past2.astype(BF16)).astype(BF16)
    fin_out[1] = dot(pick, past1.astype(BF16)).astype(BF16)
    fin_out[2] = dot(pick, new).astype(BF16)


def group_columns(blocks, low):
    b_cols, c_cols = [], []
    for q in range(4):
        part = jnp.zeros((ROWS, 128), F32)
        for k in range(4):
            part = part + jnp.where(low == (q ^ k), blocks[k], 0.0)
        b_cols.append(part[:, 0:64])
        c_cols.append(part[:, 64:128])
    return jnp.concatenate(b_cols, 1).astype(BF16), jnp.concatenate(c_cols, 1).astype(BF16)


def scan_kernel(
    par, new, conv, bc0, bc1, bc2, bc3, dt_raw, norm_gain, a_log, dt_bias, d_skip, *refs
):
    parts, (send_out, b_out, coef_out, first_out) = refs[:8], refs[8:12]
    state, send, b_buf, coef_buf, first_buf, sem_in, sem_send = refs[12:]
    head = lax.axis_index("beam")
    loads = [pltpu.make_async_copy(parts[k], state.at[pl.ds((head ^ k) * 4, 4)], sem_in.at[k]) for k in range(8)]
    for load in loads:
        load.start()
    low = lax.axis_index("row") & 3
    blocks = [ref[...].astype(F32) for ref in (bc0, bc1, bc2, bc3)]
    b_in, c_out = group_columns(blocks, low)
    t, a1, a2, a3, g = lineage(par[...])
    raw = dt_raw[...].astype(BF16).astype(F32) + head_value(dt_bias)
    step_size = jnp.maximum(raw, 0.0) + jnp.log1p(jnp.exp(-jnp.abs(raw)))
    rate = jnp.exp(head_value(a_log))
    log_decay = -rate * step_size
    rr = lax.broadcasted_iota(jnp.int32, (ROWS, ROWS), 0)
    cc = lax.broadcasted_iota(jnp.int32, (ROWS, ROWS), 1)
    eye = jnp.where(rr == cc, 1.0, 0.0)
    path1 = jnp.sum(eye * log_decay, axis=1, keepdims=True)
    path2 = path1 + jnp.sum(a1 * log_decay, axis=1, keepdims=True)
    path3 = path2 + jnp.sum(a2 * log_decay, axis=1, keepdims=True)
    path4 = path3 + jnp.sum(a3 * log_decay, axis=1, keepdims=True)
    coef = (eye + a1 * jnp.exp(path1) + a2 * jnp.exp(path2) + a3 * jnp.exp(path3)) * step_size
    first = jnp.exp(path4)
    x_conv = conv[:, 0:64]
    inner = dot_t(c_out, b_in) * coef
    read = jnp.dot(inner, x_conv.astype(F32), precision=lax.Precision.HIGHEST, preferred_element_type=F32)
    lanes_i = lax.broadcasted_iota(jnp.int32, (ROWS, BEAMS), 1).astype(F32)
    origin = jnp.sum(g * lanes_i, axis=1, keepdims=True)
    half = jnp.where(lax.broadcasted_iota(jnp.int32, (ROWS, 128), 1) < 64, 0.0, 1.0)
    origin_b = jnp.broadcast_to(origin, (ROWS, 128)) - half
    acc = jnp.zeros((ROWS, 128), F32)
    for load in loads:
        load.wait()
    for p in range(BEAMS // 2):
        both = state[2 * p : 2 * p + 2].reshape(2 * HD, NS)
        acc = acc + jnp.where(origin_b == float(2 * p), dot_t(c_out, both), 0.0)
    old = acc[:, 0:64] + acc[:, 64:128]
    x_val = x_conv.astype(F32)
    read = read + first * old + head_value(d_skip) * x_val
    gate = new[:, 64:128].astype(F32)
    gated = read * (gate / (1.0 + jnp.exp(-gate)))
    square = jnp.sum(gated * gated, axis=1, keepdims=True)
    high = square.astype(BF16).astype(F32)
    rest = square - high
    lane = lax.broadcasted_iota(jnp.int32, (ROWS, 64), 1)
    stats = jnp.where(lane == 0, high, jnp.where(lane == 1, rest, 0.0))
    send[...] = jnp.concatenate([gated * head_part(norm_gain, HD), stats], axis=1).astype(BF16)
    sends = [pltpu.make_async_copy(send, send_out.at[k], sem_send.at[k]) for k in range(8)]
    for copy in sends:
        copy.start()
    b_buf[...] = b_in
    coef_buf[...] = coef
    first_buf[...] = jnp.broadcast_to(first, (ROWS, 128))
    for n, (buf, ref) in enumerate(((b_buf, b_out), (coef_buf, coef_out), (first_buf, first_out))):
        sends.append(pltpu.make_async_copy(buf, ref, sem_send.at[8 + n]))
        sends[-1].start()
    for copy in sends:
        copy.wait()


def final_kernel(parents, conv, b_in, coef_ref, first_ref, fin, *refs):
    parts, homes = refs[:8], refs[8:16]
    state, block, sem_in, sem_home = refs[16:]
    head = lax.axis_index("beam")
    loads = [pltpu.make_async_copy(parts[k], state.at[pl.ds((head ^ k) * 4, 4)], sem_in.at[k]) for k in range(8)]
    for load in loads:
        load.start()
    x_t = conv[...].astype(F32).T[0:HD]
    for load in loads:
        load.wait()
    for i in range(8):
        for j in range(4):
            s, beam = j // 2, 2 * i + j % 2
            row = row_of(STEPS - 1, s, beam)
            at = beam
            for step in range(STEPS - 1, -1, -1):
                at = parents[step * BEAMS + s * WIDTH + at]
            origin_s = (at >> 1) * 4 + s * 2 + (at & 1)
            left = (x_t * coef_ref[row : row + 1, :]).astype(BF16)
            keep = jnp.broadcast_to(first_ref[row : row + 1, 0:1], (HD, NS))
            value = keep * state[origin_s].astype(F32) + dot(left, b_in[...])
            block[i, HD * j : HD * j + HD, :] = value.astype(BF16)
        taps = [fin[k, 4 * i : 4 * i + 4, 0:64].astype(F32) for k in range(3)]
        tail = jnp.concatenate(taps + [jnp.zeros((4, 64), F32)], axis=1)
        block[i, 4 * HD : 4 * HD + 16, :] = jnp.concatenate([tail, jnp.zeros((12, NS), F32)], axis=0).astype(BF16)
    saves = [pltpu.make_async_copy(block.at[head ^ k], homes[k], sem_home.at[k]) for k in range(8)]
    for copy in saves:
        copy.start()
    for copy in saves:
        copy.wait()


def unpack_kernel(*refs):
    parts, (ssm_out, conv_out), (tails, sem_out) = refs[:8], refs[8:10], refs[10:]
    head = lax.axis_index("beam")
    copies = []
    for k in range(8):
        for j in range(4):
            src = parts[k].at[pl.ds(HD * j, HD)]
            copies.append(pltpu.make_async_copy(src, ssm_out.at[j // 2, j % 2, head ^ k], sem_out.at[k, j]))
            copies[-1].start()
        tails[head ^ k] = parts[k][4 * HD : 4 * HD + 16, :].astype(F32)
    for h in range(8):
        tail = tails[h]
        for j in range(4):
            for k in range(3):
                conv_out[j // 2, j % 2, k, h : h + 1, :] = tail[j : j + 1, HD * k : HD * k + HD].astype(BF16)
    for copy in copies:
        copy.wait()


def out_kernel(recv, w_out, out):
    stats = recv[0, :, 64:128].astype(F32)
    for i in range(1, 8):
        stats = stats + recv[i, :, 64:128].astype(F32)
    square = stats[:, 0:1] + stats[:, 1:2]
    high = square.astype(BF16).astype(F32)
    rest = square - high
    lane = lax.broadcasted_iota(jnp.int32, (ROWS, 128), 1)
    tail = jnp.where(lane == 0, high, jnp.where(lane == 1, rest, 0.0))
    left = jnp.concatenate([recv[i, :, 0:64] for i in range(8)], axis=1)
    full = jnp.concatenate([dot(left, w_out[...]), tail], axis=1)
    for q in range(4):
        for m in range(8):
            out[4 * m + q] = full[32 * q + 4 * m : 32 * q + 4 * m + 4].astype(BF16)


def norm_kernel(recv, out):
    result = jnp.zeros((STEPS, 1024), F32)
    for g in range(8):
        total = recv[4 * g].astype(F32)
        for j in range(1, 4):
            total = total + recv[4 * g + j].astype(F32)
        square = total[:, 1024:1025] + total[:, 1025:1026]
        result = result + total[:, 0:1024] * lax.rsqrt(square * (1.0 / GROUP_CH) + EPS)
    out[...] = result.astype(BF16)


VM = pl.BlockSpec(memory_space=pltpu.VMEM)
SM = pl.BlockSpec(memory_space=pltpu.SMEM)
ANY = pl.BlockSpec(memory_space=pl.ANY)
FAR = pl.BlockSpec(memory_space=pltpu.HBM)


def call(kernel, name, specs, outs, scratch=(), mib=6, out_specs=None):
    def build(*args):
        far = [n for n, spec in enumerate(specs) if spec is FAR]
        count = len(specs)
        buffers = [pltpu.VMEM(args[n].shape, args[n].dtype) for n in far]
        sems = [pltpu.SemaphoreType.DMA((len(far),))] if far else []

        def body(*refs):
            ins = list(refs[:count])
            rest = refs[count : count + len(outs) + len(scratch)]
            held = refs[count + len(outs) + len(scratch) :]
            copies = [pltpu.make_async_copy(ins[n], held[k], held[-1].at[k]) for k, n in enumerate(far)]
            for copy in copies:
                copy.start()
            for copy in copies:
                copy.wait()
            for k, n in enumerate(far):
                ins[n] = held[k]
            kernel(*ins, *rest)

        args = [
            pltpu.with_memory_space_constraint(arg, pltpu.HBM) if specs[n] in (ANY, FAR) else arg
            for n, arg in enumerate(args)
        ]
        return pl.pallas_call(
            body,
            name=name,
            in_specs=list(specs),
            out_specs=tuple(out_specs or [VM for _ in outs]),
            out_shape=tuple(
                pltpu.HBM(s, d) if out_specs and out_specs[n] is ANY else jax.ShapeDtypeStruct(s, d)
                for n, (s, d) in enumerate(outs)
            ),
            scratch_shapes=list(scratch) + buffers + sems,
            compiler_params=pltpu.CompilerParams(vmem_limit_bytes=mib << 20),
        )(*args)

    return build


def swap(value, axis, count, mask):
    return lax.ppermute(value, axis, [(i, i ^ mask) for i in range(count)])


def local(
    x_in,
    w_inner,
    w_bc,
    w_dt,
    conv_x_w,
    conv_bc_w,
    dt_bias,
    a_log,
    d_skip,
    norm_gain,
    w_out,
    ssm_state,
    conv_x_state,
    conv_bc_state,
    parents,
):
    beam = lax.axis_index("beam")
    d_local = x_in.shape[-1]
    heads = ssm_state.shape[2]
    parent_column = parents.reshape(STEPS, 8, 4).transpose(2, 1, 0).reshape(ROWS, 1)
    x = x_in.reshape(STEPS, 8, 4, d_local).transpose(2, 1, 0, 3).reshape(ROWS, d_local)

    inner = jnp.einsum("rd,dzk->rzk", x, w_inner, preferred_element_type=F32).astype(BF16)
    inner = inner[:, ::-1].reshape(ROWS, 2, heads, HD).transpose(2, 0, 1, 3).reshape(heads, ROWS, 2 * HD)
    bc = jnp.einsum("rd,dzk->rzk", x, w_bc, preferred_element_type=F32).astype(BF16).reshape(ROWS, 128)
    top = jnp.concatenate([inner, jnp.broadcast_to(bc[None], (heads, ROWS, 128))], axis=2)
    dt = jnp.einsum("dh,rd->hr", w_dt, x, preferred_element_type=F32)
    dt_high = lax.reduce_precision(dt, 8, 7)
    dt_row = jnp.concatenate([dt_high, dt - dt_high], axis=1).astype(BF16)[:, None]
    taps_x = conv_x_state.transpose(2, 4, 0, 1, 3).reshape(heads, 12, HD)
    taps_bc = jnp.broadcast_to(conv_bc_state.transpose(2, 0, 1, 3, 4).reshape(1, 12, 128), (heads, 12, 128))
    extra = jnp.concatenate([taps_x, jnp.zeros((heads, 12, HD), BF16), taps_bc], axis=2)
    bottom = jnp.concatenate([extra, dt_row, jnp.zeros((heads, 3, 256), BF16)], axis=1)
    payload = jnp.concatenate([top, bottom], axis=1)
    recv = lax.all_to_all(payload, "beam", split_axis=0, concat_axis=0, tiled=True)

    packed = call(
        pack_kernel,
        "pack",
        [ANY],
        [((4, HD, NS), BF16)] * 8,
        [
            pltpu.VMEM((8, 4, HD, NS), BF16),
            pltpu.SemaphoreType.DMA((8, 4)),
            pltpu.SemaphoreType.DMA((8,)),
        ],
        out_specs=[ANY] * 8,
    )(ssm_state)
    states = [packed[0]] + [swap(packed[k], "beam", 8, k) for k in range(1, 8)]

    new, conv, bc_conv, dt_raw, fin = call(
        conv_kernel,
        "conv",
        [FAR, VM, VM, VM],
        [((ROWS, 256), BF16), ((ROWS, 128), BF16), ((ROWS, 128), BF16), ((1, ROWS), F32), ((3, BEAMS, 256), BF16)],
        [pltpu.VMEM((3, BEAMS, 256), F32)],
    )(recv, parent_column, conv_x_w, conv_bc_w.reshape(4, 128))

    others = [swap(bc_conv, "row", 32, k) for k in (1, 2, 3)]

    send, b_in, coef, first = call(
        scan_kernel,
        "scan",
        [VM] * 12 + [ANY] * 8,
        [((8, ROWS, 128), BF16), ((ROWS, NS), BF16), ((ROWS, ROWS), F32), ((ROWS, 128), F32)],
        [
            pltpu.VMEM((BEAMS, HD, NS), BF16),
            pltpu.VMEM((ROWS, 128), BF16),
            pltpu.VMEM((ROWS, NS), BF16),
            pltpu.VMEM((ROWS, ROWS), F32),
            pltpu.VMEM((ROWS, 128), F32),
            pltpu.SemaphoreType.DMA((8,)),
            pltpu.SemaphoreType.DMA((11,)),
        ],
        out_specs=[ANY] * 4,
    )(
        parent_column,
        new,
        conv,
        bc_conv,
        *others,
        dt_raw,
        norm_gain.reshape(1, 512),
        a_log.reshape(1, 8),
        dt_bias.reshape(1, 8),
        d_skip.reshape(1, 8),
        *states,
    )
    gathered = lax.all_to_all(send, "beam", split_axis=0, concat_axis=0, tiled=True)
    final = call(
        final_kernel,
        "final",
        [SM, VM] + [FAR] * 4 + [ANY] * 8,
        [((4 * HD + 16, NS), BF16)] * 8,
        [
            pltpu.VMEM((BEAMS, HD, NS), BF16),
            pltpu.VMEM((8, 4 * HD + 16, NS), BF16),
            pltpu.SemaphoreType.DMA((8,)),
            pltpu.SemaphoreType.DMA((8,)),
        ],
        out_specs=[ANY] * 8,
    )(parents.reshape(ROWS), conv, b_in, coef, first, fin, *states)
    homes = [final[0]] + [swap(final[k], "beam", 8, k) for k in range(1, 8)]
    gathered, homes[1] = lax.optimization_barrier((gathered, homes[1]))
    ssm_final, conv_x_rows = call(
        unpack_kernel,
        "unpack",
        [VM] * 8,
        [((SESS, 2, heads, HD, NS), BF16), ((SESS, 2, 3, heads, HD), BF16)],
        [
            pltpu.VMEM((8, 16, NS), F32),
            pltpu.SemaphoreType.DMA((8, 4)),
        ],
        out_specs=[ANY, VM],
    )(*homes)
    conv_x_final = conv_x_rows.transpose(0, 1, 3, 4, 2)

    (parts,) = call(
        out_kernel,
        "project",
        [VM, VM],
        [((BEAMS, STEPS, 1152), BF16)],
    )(gathered, w_out)
    spread = lax.all_to_all(parts, "row", split_axis=0, concat_axis=0, tiled=True)
    (layer_out,) = call(norm_kernel, "norm", [VM], [((STEPS, 1024), BF16)])(spread)
    layer_out = layer_out[:, None]

    own = lax.dynamic_slice_in_dim(fin, beam * 4, 4, 1)[:, :, 128:]
    conv_bc_final = own.reshape(3, SESS, 2, 2, 64).transpose(1, 2, 0, 3, 4)
    return layer_out, ssm_final, conv_x_final, conv_bc_final


def solution(mesh):
    placed = (
        P(None, None, None, "beam"),
        P("beam", None, "row"),
        P("beam", None, "row"),
        P("beam", "row"),
        P(None, "row"),
        P(None, None, "row"),
        P("row"),
        P("row"),
        P("row"),
        P("row"),
        P("row", "beam"),
        P(None, "beam", "row", None, None),
        P(None, "beam", "row", None, None),
        P(None, "beam", None, None, "row"),
        P(),
    )
    return jax.shard_map(
        local,
        mesh=mesh,
        in_specs=placed,
        out_specs=(
            P(None, "row", "beam"),
            P(None, "beam", "row", None, None),
            P(None, "beam", "row", None, None),
            P(None, "beam", None, None, "row"),
        ),
        check_vma=False,
    )
```

```python
import jax
import jax.numpy as jnp
from jax import lax
from jax.experimental import pallas as pl
from jax.experimental.pallas import tpu as pltpu
from jax.sharding import PartitionSpec as P

EPS = 1e-05
F32 = jnp.float32
BF16 = jnp.bfloat16
STEPS = 4
SESS = 2
WIDTH = 16
BEAMS = SESS * WIDTH
ROWS = STEPS * BEAMS
HD = 64
NS = 256
GROUP_CH = 2048.0


def row_of(step, s, b):
    v = s * WIDTH + b
    return (v % 4) * 32 + (v // 4) * 4 + step


def dot(a, b):
    return jnp.dot(a, b, preferred_element_type=F32)


def dot_t(a, b):
    return lax.dot_general(a, b, (((1,), (1,)), ((), ())), preferred_element_type=F32)


def lineage(par):
    r = lax.broadcasted_iota(jnp.int32, (ROWS, 1), 0)
    t = r & 3
    s = (r & 31) >> 4
    before = (par & 3) * 32 + (s * 4 + (par >> 2)) * 4 + t - 1
    before = jnp.where(t > 0, before, -1)
    start = jnp.where(t == 0, (par >> 1) * 4 + s * 2 + (par & 1), -1)
    lanes = lax.broadcasted_iota(jnp.int32, (ROWS, ROWS), 1)
    a1 = jnp.where(lanes == before, 1.0, 0.0)
    lanes_i = lax.broadcasted_iota(jnp.int32, (ROWS, BEAMS), 1)
    g = jnp.where(lanes_i == start, 1.0, 0.0)
    a1b = a1.astype(BF16)
    a2 = dot(a1b, a1b)
    a3 = dot(a1b, a2.astype(BF16))
    gb = g.astype(BF16)
    g1 = dot(a1b, gb)
    g2 = dot(a1b, g1.astype(BF16))
    g3 = dot(a1b, g2.astype(BF16))
    return t, a1, a2, a3, g + g1 + g2 + g3


def head_part(ref, width):
    head = lax.axis_index("beam")
    part = jnp.zeros((ref.shape[0], width), F32)
    for h in range(8):
        part = part + jnp.where(head == h, ref[:, width * h : width * h + width].astype(F32), 0.0)
    return part


def head_value(ref):
    lane = lax.broadcasted_iota(jnp.int32, (1, 8), 1)
    return jnp.sum(jnp.where(lane == lax.axis_index("beam"), ref[...], 0.0), axis=1, keepdims=True)


def pack_kernel(state, *refs):
    outs, (held, sem_in, sem_out) = refs[:8], refs[8:]
    head = lax.axis_index("beam")
    loads = []
    for k in range(8):
        for j in range(4):
            loads.append(pltpu.make_async_copy(state.at[j // 2, j % 2, head ^ k], held.at[k, j], sem_in.at[k, j]))
            loads[-1].start()
    copies = []
    for k in range(8):
        for j in range(4):
            loads[4 * k + j].wait()
        copies.append(pltpu.make_async_copy(held.at[k], outs[k], sem_out.at[k]))
        copies[-1].start()
    for copy in copies:
        copy.wait()


def conv_kernel(recv, par, conv_x_w, conv_bc_w, sum_out, conv_out, bc_out, dt_out, fin_out, init):
    total = recv[0, 0:ROWS, :].astype(F32)
    dt = recv[0, 128:144, :].astype(F32)
    for k in range(3):
        init[k, 0:4, :] = dt[4 * k : 4 * k + 4]
    for i in range(1, 8):
        total = total + recv[i, 0:ROWS, :].astype(F32)
        extra = recv[i, 128:144, :].astype(F32)
        for k in range(3):
            init[k, 4 * i : 4 * i + 4, :] = extra[4 * k : 4 * k + 4]
        dt = dt + extra
    dt_out[...] = dt[12:13, 0:128] + dt[12:13, 128:256]
    new = total.astype(BF16)
    t, a1, a2, a3, g = lineage(par[...])
    gb = g.astype(BF16)
    start = [dot(gb, init[k].astype(BF16)) for k in range(3)]
    past1 = dot(a1.astype(BF16), new) + jnp.where(t == 0, start[2], 0.0)
    past2 = dot(a2.astype(BF16), new) + jnp.where(t == 0, start[1], 0.0) + jnp.where(t == 1, start[2], 0.0)
    past3 = (
        dot(a3.astype(BF16), new)
        + jnp.where(t == 0, start[0], 0.0)
        + jnp.where(t == 1, start[1], 0.0)
        + jnp.where(t == 2, start[2], 0.0)
    )
    w = jnp.concatenate([head_part(conv_x_w, HD), jnp.zeros((4, HD), F32), conv_bc_w[...].astype(F32)], axis=1)
    mixed = w[0:1] * past3 + w[1:2] * past2 + w[2:3] * past1 + w[3:4] * new.astype(F32)
    conv = mixed / (1.0 + jnp.exp(-mixed))
    sum_out[...] = new
    conv_out[...] = conv[:, 0:128].astype(BF16)
    bc_out[...] = conv[:, 128:256].astype(BF16)
    e = lax.broadcasted_iota(jnp.int32, (BEAMS, ROWS), 0)
    b = (e >> 2) * 2 + (e & 1)
    s = (e >> 1) & 1
    last = (b & 3) * 32 + (s * 4 + (b >> 2)) * 4 + STEPS - 1
    pick = jnp.where(lax.broadcasted_iota(jnp.int32, (BEAMS, ROWS), 1) == last, 1.0, 0.0).astype(BF16)
    fin_out[0] = dot(pick, past2.astype(BF16)).astype(BF16)
    fin_out[1] = dot(pick, past1.astype(BF16)).astype(BF16)
    fin_out[2] = dot(pick, new).astype(BF16)


def group_columns(blocks, low):
    b_cols, c_cols = [], []
    for q in range(4):
        part = jnp.zeros((ROWS, 128), F32)
        for k in range(4):
            part = part + jnp.where(low == (q ^ k), blocks[k], 0.0)
        b_cols.append(part[:, 0:64])
        c_cols.append(part[:, 64:128])
    return jnp.concatenate(b_cols, 1).astype(BF16), jnp.concatenate(c_cols, 1).astype(BF16)


def scan_kernel(
    par, new, conv, bc0, bc1, bc2, bc3, dt_raw, norm_gain, a_log, dt_bias, d_skip, *refs
):
    parts, (send_out, b_out, coef_out, first_out) = refs[:8], refs[8:12]
    state, send, b_buf, coef_buf, first_buf, sem_in, sem_send = refs[12:]
    head = lax.axis_index("beam")
    loads = [pltpu.make_async_copy(parts[k], state.at[pl.ds((head ^ k) * 4, 4)], sem_in.at[k]) for k in range(8)]
    for load in loads:
        load.start()
    low = lax.axis_index("row") & 3
    blocks = [ref[...].astype(F32) for ref in (bc0, bc1, bc2, bc3)]
    b_in, c_out = group_columns(blocks, low)
    t, a1, a2, a3, g = lineage(par[...])
    raw = dt_raw[...].astype(BF16).astype(F32) + head_value(dt_bias)
    step_size = jnp.maximum(raw, 0.0) + jnp.log1p(jnp.exp(-jnp.abs(raw)))
    rate = jnp.exp(head_value(a_log))
    log_decay = -rate * step_size
    rr = lax.broadcasted_iota(jnp.int32, (ROWS, ROWS), 0)
    cc = lax.broadcasted_iota(jnp.int32, (ROWS, ROWS), 1)
    eye = jnp.where(rr == cc, 1.0, 0.0)
    path1 = jnp.sum(eye * log_decay, axis=1, keepdims=True)
    path2 = path1 + jnp.sum(a1 * log_decay, axis=1, keepdims=True)
    path3 = path2 + jnp.sum(a2 * log_decay, axis=1, keepdims=True)
    path4 = path3 + jnp.sum(a3 * log_decay, axis=1, keepdims=True)
    coef = (eye + a1 * jnp.exp(path1) + a2 * jnp.exp(path2) + a3 * jnp.exp(path3)) * step_size
    first = jnp.exp(path4)
    x_conv = conv[:, 0:64]
    inner = dot_t(c_out, b_in) * coef
    read = jnp.dot(inner, x_conv.astype(F32), precision=lax.Precision.HIGHEST, preferred_element_type=F32)
    lanes_i = lax.broadcasted_iota(jnp.int32, (ROWS, BEAMS), 1).astype(F32)
    origin = jnp.sum(g * lanes_i, axis=1, keepdims=True)
    half = jnp.where(lax.broadcasted_iota(jnp.int32, (ROWS, 128), 1) < 64, 0.0, 1.0)
    origin_b = jnp.broadcast_to(origin, (ROWS, 128)) - half
    acc = jnp.zeros((ROWS, 128), F32)
    for load in loads:
        load.wait()
    for p in range(BEAMS // 2):
        both = state[2 * p : 2 * p + 2].reshape(2 * HD, NS)
        acc = acc + jnp.where(origin_b == float(2 * p), dot_t(c_out, both), 0.0)
    old = acc[:, 0:64] + acc[:, 64:128]
    x_val = x_conv.astype(F32)
    read = read + first * old + head_value(d_skip) * x_val
    gate = new[:, 64:128].astype(F32)
    gated = read * (gate / (1.0 + jnp.exp(-gate)))
    square = jnp.sum(gated * gated, axis=1, keepdims=True)
    high = square.astype(BF16).astype(F32)
    rest = square - high
    lane = lax.broadcasted_iota(jnp.int32, (ROWS, 64), 1)
    stats = jnp.where(lane == 0, high, jnp.where(lane == 1, rest, 0.0))
    send[...] = jnp.concatenate([gated * head_part(norm_gain, HD), stats], axis=1).astype(BF16)
    sends = [pltpu.make_async_copy(send, send_out.at[k], sem_send.at[k]) for k in range(8)]
    for copy in sends:
        copy.start()
    b_buf[...] = b_in
    coef_buf[...] = coef
    first_buf[...] = jnp.broadcast_to(first, (ROWS, 128))
    for n, (buf, ref) in enumerate(((b_buf, b_out), (coef_buf, coef_out), (first_buf, first_out))):
        sends.append(pltpu.make_async_copy(buf, ref, sem_send.at[8 + n]))
        sends[-1].start()
    for copy in sends:
        copy.wait()


def final_kernel(parents, conv, b_in, coef_ref, first_ref, fin, *refs):
    parts, homes = refs[:8], refs[8:16]
    state, block, sem_in, sem_home = refs[16:]
    head = lax.axis_index("beam")
    loads = [pltpu.make_async_copy(parts[k], state.at[pl.ds((head ^ k) * 4, 4)], sem_in.at[k]) for k in range(8)]
    for load in loads:
        load.start()
    x_t = conv[...].astype(F32).T[0:HD]
    b = b_in[...]
    for load in loads:
        load.wait()
    saves = []
    for i in range(8):
        rows = [row_of(STEPS - 1, j // 2, 2 * i + j % 2) for j in range(4)]
        left = jnp.concatenate([x_t * coef_ref[row : row + 1, :] for row in rows], axis=0).astype(BF16)
        update = dot(left, b)
        for j in range(4):
            s, at = j // 2, 2 * i + j % 2
            for step in range(STEPS - 1, -1, -1):
                at = parents[step * BEAMS + s * WIDTH + at]
            origin = (at >> 1) * 4 + s * 2 + (at & 1)
            keep = jnp.broadcast_to(first_ref[rows[j] : rows[j] + 1, 0:1], (HD, NS))
            value = keep * state[origin].astype(F32) + update[HD * j : HD * j + HD]
            block[i, HD * j : HD * j + HD, :] = value.astype(BF16)
        taps = [fin[k, 4 * i : 4 * i + 4, 0:64].astype(F32) for k in range(3)]
        tail = jnp.concatenate(taps + [jnp.zeros((4, 64), F32)], axis=1)
        block[i, 4 * HD : 4 * HD + 16, :] = jnp.concatenate([tail, jnp.zeros((12, NS), F32)], axis=0).astype(BF16)
    for k in range(8):
        saves.append(pltpu.make_async_copy(block.at[head ^ k], homes[k], sem_home.at[k]))
        saves[-1].start()
    for copy in saves:
        copy.wait()


def unpack_kernel(*refs):
    parts, (ssm_out, conv_out), (tails, sem_out) = refs[:8], refs[8:10], refs[10:]
    head = lax.axis_index("beam")
    copies = []
    for k in range(8):
        for j in range(4):
            src = parts[k].at[pl.ds(HD * j, HD)]
            copies.append(pltpu.make_async_copy(src, ssm_out.at[j // 2, j % 2, head ^ k], sem_out.at[k, j]))
            copies[-1].start()
        tails[head ^ k] = parts[k][4 * HD : 4 * HD + 16, :].astype(F32)
    for h in range(8):
        tail = tails[h]
        for j in range(4):
            for k in range(3):
                conv_out[j // 2, j % 2, k, h : h + 1, :] = tail[j : j + 1, HD * k : HD * k + HD].astype(BF16)
    for copy in copies:
        copy.wait()


def out_kernel(recv, w_out, out):
    stats = recv[0, :, 64:128].astype(F32)
    for i in range(1, 8):
        stats = stats + recv[i, :, 64:128].astype(F32)
    square = stats[:, 0:1] + stats[:, 1:2]
    high = square.astype(BF16).astype(F32)
    rest = square - high
    lane = lax.broadcasted_iota(jnp.int32, (ROWS, 128), 1)
    tail = jnp.where(lane == 0, high, jnp.where(lane == 1, rest, 0.0))
    left = jnp.concatenate([recv[i, :, 0:64] for i in range(8)], axis=1)
    full = jnp.concatenate([dot(left, w_out[...]), tail], axis=1)
    for q in range(4):
        for m in range(8):
            out[4 * m + q] = full[32 * q + 4 * m : 32 * q + 4 * m + 4].astype(BF16)


def norm_kernel(recv, out):
    result = jnp.zeros((STEPS, 1024), F32)
    for g in range(8):
        total = recv[4 * g].astype(F32)
        for j in range(1, 4):
            total = total + recv[4 * g + j].astype(F32)
        square = total[:, 1024:1025] + total[:, 1025:1026]
        result = result + total[:, 0:1024] * lax.rsqrt(square * (1.0 / GROUP_CH) + EPS)
    out[...] = result.astype(BF16)


VM = pl.BlockSpec(memory_space=pltpu.VMEM)
SM = pl.BlockSpec(memory_space=pltpu.SMEM)
ANY = pl.BlockSpec(memory_space=pl.ANY)
FAR = pl.BlockSpec(memory_space=pltpu.HBM)


def call(kernel, name, specs, outs, scratch=(), mib=6, out_specs=None):
    def build(*args):
        far = [n for n, spec in enumerate(specs) if spec is FAR]
        count = len(specs)
        buffers = [pltpu.VMEM(args[n].shape, args[n].dtype) for n in far]
        sems = [pltpu.SemaphoreType.DMA((len(far),))] if far else []

        def body(*refs):
            ins = list(refs[:count])
            rest = refs[count : count + len(outs) + len(scratch)]
            held = refs[count + len(outs) + len(scratch) :]
            copies = [pltpu.make_async_copy(ins[n], held[k], held[-1].at[k]) for k, n in enumerate(far)]
            for copy in copies:
                copy.start()
            for copy in copies:
                copy.wait()
            for k, n in enumerate(far):
                ins[n] = held[k]
            kernel(*ins, *rest)

        args = [
            pltpu.with_memory_space_constraint(arg, pltpu.HBM) if specs[n] in (ANY, FAR) else arg
            for n, arg in enumerate(args)
        ]
        return pl.pallas_call(
            body,
            name=name,
            in_specs=list(specs),
            out_specs=tuple(out_specs or [VM for _ in outs]),
            out_shape=tuple(
                pltpu.HBM(s, d) if out_specs and out_specs[n] is ANY else jax.ShapeDtypeStruct(s, d)
                for n, (s, d) in enumerate(outs)
            ),
            scratch_shapes=list(scratch) + buffers + sems,
            compiler_params=pltpu.CompilerParams(vmem_limit_bytes=mib << 20),
        )(*args)

    return build


def swap(value, axis, count, mask):
    return lax.ppermute(value, axis, [(i, i ^ mask) for i in range(count)])


def local(
    x_in,
    w_inner,
    w_bc,
    w_dt,
    conv_x_w,
    conv_bc_w,
    dt_bias,
    a_log,
    d_skip,
    norm_gain,
    w_out,
    ssm_state,
    conv_x_state,
    conv_bc_state,
    parents,
):
    beam = lax.axis_index("beam")
    d_local = x_in.shape[-1]
    heads = ssm_state.shape[2]
    parent_column = parents.reshape(STEPS, 8, 4).transpose(2, 1, 0).reshape(ROWS, 1)
    x = x_in.reshape(STEPS, 8, 4, d_local).transpose(2, 1, 0, 3).reshape(ROWS, d_local)

    inner = jnp.einsum("rd,dzk->rzk", x, w_inner, preferred_element_type=F32).astype(BF16)
    inner = inner[:, ::-1].reshape(ROWS, 2, heads, HD).transpose(2, 0, 1, 3).reshape(heads, ROWS, 2 * HD)
    bc = jnp.einsum("rd,dzk->rzk", x, w_bc, preferred_element_type=F32).astype(BF16).reshape(ROWS, 128)
    top = jnp.concatenate([inner, jnp.broadcast_to(bc[None], (heads, ROWS, 128))], axis=2)
    dt = jnp.einsum("dh,rd->hr", w_dt, x, preferred_element_type=F32)
    dt_high = lax.reduce_precision(dt, 8, 7)
    dt_row = jnp.concatenate([dt_high, dt - dt_high], axis=1).astype(BF16)[:, None]
    taps_x = conv_x_state.transpose(2, 4, 0, 1, 3).reshape(heads, 12, HD)
    taps_bc = jnp.broadcast_to(conv_bc_state.transpose(2, 0, 1, 3, 4).reshape(1, 12, 128), (heads, 12, 128))
    extra = jnp.concatenate([taps_x, jnp.zeros((heads, 12, HD), BF16), taps_bc], axis=2)
    bottom = jnp.concatenate([extra, dt_row, jnp.zeros((heads, 3, 256), BF16)], axis=1)
    payload = jnp.concatenate([top, bottom], axis=1)
    recv = lax.all_to_all(payload, "beam", split_axis=0, concat_axis=0, tiled=True)

    packed = call(
        pack_kernel,
        "pack",
        [ANY],
        [((4, HD, NS), BF16)] * 8,
        [
            pltpu.VMEM((8, 4, HD, NS), BF16),
            pltpu.SemaphoreType.DMA((8, 4)),
            pltpu.SemaphoreType.DMA((8,)),
        ],
        out_specs=[ANY] * 8,
    )(ssm_state)
    states = [packed[0]] + [swap(packed[k], "beam", 8, k) for k in range(1, 8)]

    new, conv, bc_conv, dt_raw, fin = call(
        conv_kernel,
        "conv",
        [FAR, VM, VM, VM],
        [((ROWS, 256), BF16), ((ROWS, 128), BF16), ((ROWS, 128), BF16), ((1, ROWS), F32), ((3, BEAMS, 256), BF16)],
        [pltpu.VMEM((3, BEAMS, 256), F32)],
    )(recv, parent_column, conv_x_w, conv_bc_w.reshape(4, 128))

    others = [swap(bc_conv, "row", 32, k) for k in (1, 2, 3)]

    send, b_in, coef, first = call(
        scan_kernel,
        "scan",
        [VM] * 12 + [ANY] * 8,
        [((8, ROWS, 128), BF16), ((ROWS, NS), BF16), ((ROWS, ROWS), F32), ((ROWS, 128), F32)],
        [
            pltpu.VMEM((BEAMS, HD, NS), BF16),
            pltpu.VMEM((ROWS, 128), BF16),
            pltpu.VMEM((ROWS, NS), BF16),
            pltpu.VMEM((ROWS, ROWS), F32),
            pltpu.VMEM((ROWS, 128), F32),
            pltpu.SemaphoreType.DMA((8,)),
            pltpu.SemaphoreType.DMA((11,)),
        ],
        out_specs=[ANY] * 4,
    )(
        parent_column,
        new,
        conv,
        bc_conv,
        *others,
        dt_raw,
        norm_gain.reshape(1, 512),
        a_log.reshape(1, 8),
        dt_bias.reshape(1, 8),
        d_skip.reshape(1, 8),
        *states,
    )
    gathered = lax.all_to_all(send, "beam", split_axis=0, concat_axis=0, tiled=True)
    final = list(call(
        final_kernel,
        "final",
        [SM, VM] + [FAR] * 4 + [ANY] * 8,
        [((4 * HD + 16, NS), BF16)] * 8,
        [
            pltpu.VMEM((BEAMS, HD, NS), BF16),
            pltpu.VMEM((8, 4 * HD + 16, NS), BF16),
            pltpu.SemaphoreType.DMA((8,)),
            pltpu.SemaphoreType.DMA((8,)),
        ],
        out_specs=[ANY] * 8,
    )(parents.reshape(ROWS), conv, b_in, coef, first, fin, *states))
    gathered, *final = lax.optimization_barrier((gathered, *final))
    homes = [final[0]] + [swap(final[k], "beam", 8, k) for k in range(1, 8)]
    ssm_final, conv_x_rows = call(
        unpack_kernel,
        "unpack",
        [VM] * 8,
        [((SESS, 2, heads, HD, NS), BF16), ((SESS, 2, 3, heads, HD), BF16)],
        [
            pltpu.VMEM((8, 16, NS), F32),
            pltpu.SemaphoreType.DMA((8, 4)),
        ],
        out_specs=[ANY, VM],
    )(*homes)
    conv_x_final = conv_x_rows.transpose(0, 1, 3, 4, 2)

    (parts,) = call(
        out_kernel,
        "project",
        [VM, VM],
        [((BEAMS, STEPS, 1152), BF16)],
    )(gathered, w_out)
    spread = lax.all_to_all(parts, "row", split_axis=0, concat_axis=0, tiled=True)
    (layer_out,) = call(norm_kernel, "norm", [VM], [((STEPS, 1024), BF16)])(spread)
    layer_out = layer_out[:, None]

    own = lax.dynamic_slice_in_dim(fin, beam * 4, 4, 1)[:, :, 128:]
    conv_bc_final = own.reshape(3, SESS, 2, 2, 64).transpose(1, 2, 0, 3, 4)
    return layer_out, ssm_final, conv_x_final, conv_bc_final


def solution(mesh):
    placed = (
        P(None, None, None, "beam"),
        P("beam", None, "row"),
        P("beam", None, "row"),
        P("beam", "row"),
        P(None, "row"),
        P(None, None, "row"),
        P("row"),
        P("row"),
        P("row"),
        P("row"),
        P("row", "beam"),
        P(None, "beam", "row", None, None),
        P(None, "beam", "row", None, None),
        P(None, "beam", None, None, "row"),
        P(),
    )
    return jax.shard_map(
        local,
        mesh=mesh,
        in_specs=placed,
        out_specs=(
            P(None, "row", "beam"),
            P(None, "beam", "row", None, None),
            P(None, "beam", "row", None, None),
            P(None, "beam", None, None, "row"),
        ),
        check_vma=False,
    )
```

```python
import jax
import jax.numpy as jnp
from jax import lax
from jax.experimental import pallas as pl
from jax.experimental.pallas import tpu as pltpu
from jax.sharding import PartitionSpec as P

EPS = 1e-05
F32 = jnp.float32
BF16 = jnp.bfloat16
STEPS = 4
SESS = 2
WIDTH = 16
BEAMS = SESS * WIDTH
ROWS = STEPS * BEAMS
HD = 64
NS = 256
GROUP_CH = 2048.0


def row_of(step, s, b):
    v = s * WIDTH + b
    return (v % 4) * 32 + (v // 4) * 4 + step


def dot(a, b):
    return jnp.dot(a, b, preferred_element_type=F32)


def dot_t(a, b):
    return lax.dot_general(a, b, (((1,), (1,)), ((), ())), preferred_element_type=F32)


def lineage(par):
    r = lax.broadcasted_iota(jnp.int32, (ROWS, 1), 0)
    t = r & 3
    s = (r & 31) >> 4
    before = (par & 3) * 32 + (s * 4 + (par >> 2)) * 4 + t - 1
    before = jnp.where(t > 0, before, -1)
    start = jnp.where(t == 0, (par >> 1) * 4 + s * 2 + (par & 1), -1)
    lanes = lax.broadcasted_iota(jnp.int32, (ROWS, ROWS), 1)
    a1 = jnp.where(lanes == before, 1.0, 0.0)
    lanes_i = lax.broadcasted_iota(jnp.int32, (ROWS, BEAMS), 1)
    g = jnp.where(lanes_i == start, 1.0, 0.0)
    a1b = a1.astype(BF16)
    a2 = dot(a1b, a1b)
    a3 = dot(a1b, a2.astype(BF16))
    gb = g.astype(BF16)
    g1 = dot(a1b, gb)
    g2 = dot(a1b, g1.astype(BF16))
    g3 = dot(a1b, g2.astype(BF16))
    return t, a1, a2, a3, g + g1 + g2 + g3


def head_part(ref, width):
    head = lax.axis_index("beam")
    part = jnp.zeros((ref.shape[0], width), F32)
    for h in range(8):
        part = part + jnp.where(head == h, ref[:, width * h : width * h + width].astype(F32), 0.0)
    return part


def head_value(ref):
    lane = lax.broadcasted_iota(jnp.int32, (1, 8), 1)
    return jnp.sum(jnp.where(lane == lax.axis_index("beam"), ref[...], 0.0), axis=1, keepdims=True)


def pack_kernel(state, *refs):
    outs, sems = refs[:8], refs[8]
    head = lax.axis_index("beam")
    loads = []
    for k in range(8):
        for j in range(4):
            loads.append(pltpu.make_async_copy(state.at[j // 2, j % 2, head ^ k], outs[k].at[j], sems.at[k, j]))
            loads[-1].start()
    for load in loads:
        load.wait()


def conv_kernel(recv, par, conv_x_w, conv_bc_w, sum_out, conv_out, bc_out, dt_out, fin_out, init):
    total = recv[0, 0:ROWS, :].astype(F32)
    dt = recv[0, 128:144, :].astype(F32)
    for k in range(3):
        init[k, 0:4, :] = dt[4 * k : 4 * k + 4]
    for i in range(1, 8):
        total = total + recv[i, 0:ROWS, :].astype(F32)
        extra = recv[i, 128:144, :].astype(F32)
        for k in range(3):
            init[k, 4 * i : 4 * i + 4, :] = extra[4 * k : 4 * k + 4]
        dt = dt + extra
    r = lax.broadcasted_iota(jnp.int32, (ROWS, ROWS), 0)
    source = (r & 3) * 32 + ((r & 31) >> 2) * 4 + (r >> 5)
    order = jnp.where(lax.broadcasted_iota(jnp.int32, (ROWS, ROWS), 1) == source, 1.0, 0.0)
    dt_sum = (dt[12:13, 0:128] + dt[12:13, 128:256]).astype(BF16)
    dt_out[...] = dot_t(jnp.broadcast_to(dt_sum, (8, ROWS)), order.astype(BF16))[0:1]
    new = dot(order.astype(BF16), total.astype(BF16)).astype(BF16)
    t, a1, a2, a3, g = lineage(par[...])
    gb = g.astype(BF16)
    start = [dot(gb, init[k].astype(BF16)) for k in range(3)]
    past1 = dot(a1.astype(BF16), new) + jnp.where(t == 0, start[2], 0.0)
    past2 = dot(a2.astype(BF16), new) + jnp.where(t == 0, start[1], 0.0) + jnp.where(t == 1, start[2], 0.0)
    past3 = (
        dot(a3.astype(BF16), new)
        + jnp.where(t == 0, start[0], 0.0)
        + jnp.where(t == 1, start[1], 0.0)
        + jnp.where(t == 2, start[2], 0.0)
    )
    w = jnp.concatenate([head_part(conv_x_w, HD), jnp.zeros((4, HD), F32), conv_bc_w[...].astype(F32)], axis=1)
    mixed = w[0:1] * past3 + w[1:2] * past2 + w[2:3] * past1 + w[3:4] * new.astype(F32)
    conv = mixed / (1.0 + jnp.exp(-mixed))
    sum_out[...] = new
    conv_out[...] = conv[:, 0:128].astype(BF16)
    bc_out[...] = conv[:, 128:256].astype(BF16)
    e = lax.broadcasted_iota(jnp.int32, (BEAMS, ROWS), 0)
    b = (e >> 2) * 2 + (e & 1)
    s = (e >> 1) & 1
    last = (b & 3) * 32 + (s * 4 + (b >> 2)) * 4 + STEPS - 1
    pick = jnp.where(lax.broadcasted_iota(jnp.int32, (BEAMS, ROWS), 1) == last, 1.0, 0.0).astype(BF16)
    fin_out[0] = dot(pick, past2.astype(BF16)).astype(BF16)
    fin_out[1] = dot(pick, past1.astype(BF16)).astype(BF16)
    fin_out[2] = dot(pick, new).astype(BF16)


def group_columns(blocks, low):
    b_cols, c_cols = [], []
    for q in range(4):
        part = jnp.zeros((ROWS, 128), F32)
        for k in range(4):
            part = part + jnp.where(low == (q ^ k), blocks[k], 0.0)
        b_cols.append(part[:, 0:64])
        c_cols.append(part[:, 64:128])
    return jnp.concatenate(b_cols, 1).astype(BF16), jnp.concatenate(c_cols, 1).astype(BF16)


def scan_kernel(
    par, new, conv, bc0, bc1, bc2, bc3, dt_raw, norm_gain, a_log, dt_bias, d_skip, *refs
):
    parts, (send_out, b_out, coef_out, first_out) = refs[:8], refs[8:12]
    state, send, b_buf, coef_buf, first_buf, sem_in, sem_send = refs[12:]
    head = lax.axis_index("beam")
    loads = [pltpu.make_async_copy(parts[k], state.at[pl.ds((head ^ k) * 4, 4)], sem_in.at[k]) for k in range(8)]
    for load in loads:
        load.start()
    low = lax.axis_index("row") & 3
    blocks = [ref[...].astype(F32) for ref in (bc0, bc1, bc2, bc3)]
    b_in, c_out = group_columns(blocks, low)
    t, a1, a2, a3, g = lineage(par[...])
    raw = dt_raw[...].astype(BF16).astype(F32) + head_value(dt_bias)
    step_size = jnp.maximum(raw, 0.0) + jnp.log1p(jnp.exp(-jnp.abs(raw)))
    rate = jnp.exp(head_value(a_log))
    log_decay = -rate * step_size
    rr = lax.broadcasted_iota(jnp.int32, (ROWS, ROWS), 0)
    cc = lax.broadcasted_iota(jnp.int32, (ROWS, ROWS), 1)
    eye = jnp.where(rr == cc, 1.0, 0.0)
    path1 = jnp.sum(eye * log_decay, axis=1, keepdims=True)
    path2 = path1 + jnp.sum(a1 * log_decay, axis=1, keepdims=True)
    path3 = path2 + jnp.sum(a2 * log_decay, axis=1, keepdims=True)
    path4 = path3 + jnp.sum(a3 * log_decay, axis=1, keepdims=True)
    coef = (eye + a1 * jnp.exp(path1) + a2 * jnp.exp(path2) + a3 * jnp.exp(path3)) * step_size
    first = jnp.exp(path4)
    x_conv = conv[:, 0:64]
    inner = dot_t(c_out, b_in) * coef
    read = jnp.dot(inner, x_conv.astype(F32), precision=lax.Precision.HIGHEST, preferred_element_type=F32)
    lanes_i = lax.broadcasted_iota(jnp.int32, (ROWS, BEAMS), 1).astype(F32)
    origin = jnp.sum(g * lanes_i, axis=1, keepdims=True)
    half = jnp.where(lax.broadcasted_iota(jnp.int32, (ROWS, 128), 1) < 64, 0.0, 1.0)
    origin_b = jnp.broadcast_to(origin, (ROWS, 128)) - half
    acc = jnp.zeros((ROWS, 128), F32)
    for load in loads:
        load.wait()
    for p in range(BEAMS // 2):
        both = state[2 * p : 2 * p + 2].reshape(2 * HD, NS)
        acc = acc + jnp.where(origin_b == float(2 * p), dot_t(c_out, both), 0.0)
    old = acc[:, 0:64] + acc[:, 64:128]
    x_val = x_conv.astype(F32)
    read = read + first * old + head_value(d_skip) * x_val
    gate = new[:, 64:128].astype(F32)
    gated = read * (gate / (1.0 + jnp.exp(-gate)))
    square = jnp.sum(gated * gated, axis=1, keepdims=True)
    high = square.astype(BF16).astype(F32)
    rest = square - high
    lane = lax.broadcasted_iota(jnp.int32, (ROWS, 64), 1)
    stats = jnp.where(lane == 0, high, jnp.where(lane == 1, rest, 0.0))
    send[...] = jnp.concatenate([gated * head_part(norm_gain, HD), stats], axis=1).astype(BF16)
    sends = [pltpu.make_async_copy(send, send_out.at[k], sem_send.at[k]) for k in range(8)]
    for copy in sends:
        copy.start()
    b_buf[...] = b_in
    coef_buf[...] = coef
    first_buf[...] = jnp.broadcast_to(first, (ROWS, 128))
    for n, (buf, ref) in enumerate(((b_buf, b_out), (coef_buf, coef_out), (first_buf, first_out))):
        sends.append(pltpu.make_async_copy(buf, ref, sem_send.at[8 + n]))
        sends[-1].start()
    for copy in sends:
        copy.wait()


def final_kernel(parents, conv, b_in, coef_ref, first_ref, fin, *refs):
    parts, homes = refs[:8], refs[8:16]
    state, block, sem_in, sem_home = refs[16:]
    head = lax.axis_index("beam")
    loads = [pltpu.make_async_copy(parts[k], state.at[pl.ds((head ^ k) * 4, 4)], sem_in.at[k]) for k in range(8)]
    for load in loads:
        load.start()
    x_t = conv[...].astype(F32).T[0:HD]
    b = b_in[...]
    for load in loads:
        load.wait()
    saves = []
    for i in range(8):
        rows = [row_of(STEPS - 1, j // 2, 2 * i + j % 2) for j in range(4)]
        left = jnp.concatenate([x_t * coef_ref[row : row + 1, :] for row in rows], axis=0).astype(BF16)
        update = dot(left, b)
        for j in range(4):
            s, at = j // 2, 2 * i + j % 2
            for step in range(STEPS - 1, -1, -1):
                at = parents[step * BEAMS + s * WIDTH + at]
            origin = (at >> 1) * 4 + s * 2 + (at & 1)
            keep = jnp.broadcast_to(first_ref[rows[j] : rows[j] + 1, 0:1], (HD, NS))
            value = keep * state[origin].astype(F32) + update[HD * j : HD * j + HD]
            block[i, HD * j : HD * j + HD, :] = value.astype(BF16)
        taps = [fin[k, 4 * i : 4 * i + 4, 0:64].astype(F32) for k in range(3)]
        tail = jnp.concatenate(taps + [jnp.zeros((4, 64), F32)], axis=1)
        block[i, 4 * HD : 4 * HD + 16, :] = jnp.concatenate([tail, jnp.zeros((12, NS), F32)], axis=0).astype(BF16)
    for k in range(8):
        saves.append(pltpu.make_async_copy(block.at[head ^ k], homes[k], sem_home.at[k]))
        saves[-1].start()
    for copy in saves:
        copy.wait()


def unpack_kernel(*refs):
    parts, (ssm_out, conv_out), (tails, sem_out) = refs[:8], refs[8:10], refs[10:]
    head = lax.axis_index("beam")
    copies = []
    for k in range(8):
        for j in range(4):
            src = parts[k].at[pl.ds(HD * j, HD)]
            copies.append(pltpu.make_async_copy(src, ssm_out.at[j // 2, j % 2, head ^ k], sem_out.at[k, j]))
            copies[-1].start()
        tails[head ^ k] = parts[k][4 * HD : 4 * HD + 16, :].astype(F32)
    for h in range(8):
        tail = tails[h]
        for j in range(4):
            for k in range(3):
                conv_out[j // 2, j % 2, k, h : h + 1, :] = tail[j : j + 1, HD * k : HD * k + HD].astype(BF16)
    for copy in copies:
        copy.wait()


def out_kernel(recv, w_out, out):
    stats = recv[0, :, 64:128].astype(F32)
    for i in range(1, 8):
        stats = stats + recv[i, :, 64:128].astype(F32)
    square = stats[:, 0:1] + stats[:, 1:2]
    high = square.astype(BF16).astype(F32)
    rest = square - high
    lane = lax.broadcasted_iota(jnp.int32, (ROWS, 128), 1)
    tail = jnp.where(lane == 0, high, jnp.where(lane == 1, rest, 0.0))
    left = jnp.concatenate([recv[i, :, 0:64] for i in range(8)], axis=1)
    full = jnp.concatenate([dot(left, w_out[...]), tail], axis=1)
    for q in range(4):
        for m in range(8):
            out[4 * m + q] = full[32 * q + 4 * m : 32 * q + 4 * m + 4].astype(BF16)


def norm_kernel(recv, out):
    result = jnp.zeros((STEPS, 1024), F32)
    for g in range(8):
        total = recv[4 * g].astype(F32)
        for j in range(1, 4):
            total = total + recv[4 * g + j].astype(F32)
        square = total[:, 1024:1025] + total[:, 1025:1026]
        result = result + total[:, 0:1024] * lax.rsqrt(square * (1.0 / GROUP_CH) + EPS)
    out[...] = result.astype(BF16)


VM = pl.BlockSpec(memory_space=pltpu.VMEM)
SM = pl.BlockSpec(memory_space=pltpu.SMEM)
ANY = pl.BlockSpec(memory_space=pl.ANY)
FAR = pl.BlockSpec(memory_space=pltpu.HBM)


def call(kernel, name, specs, outs, scratch=(), mib=6, out_specs=None):
    def build(*args):
        far = [n for n, spec in enumerate(specs) if spec is FAR]
        count = len(specs)
        buffers = [pltpu.VMEM(args[n].shape, args[n].dtype) for n in far]
        sems = [pltpu.SemaphoreType.DMA((len(far),))] if far else []

        def body(*refs):
            ins = list(refs[:count])
            rest = refs[count : count + len(outs) + len(scratch)]
            held = refs[count + len(outs) + len(scratch) :]
            copies = [pltpu.make_async_copy(ins[n], held[k], held[-1].at[k]) for k, n in enumerate(far)]
            for copy in copies:
                copy.start()
            for copy in copies:
                copy.wait()
            for k, n in enumerate(far):
                ins[n] = held[k]
            kernel(*ins, *rest)

        args = [
            pltpu.with_memory_space_constraint(arg, pltpu.HBM) if specs[n] in (ANY, FAR) else arg
            for n, arg in enumerate(args)
        ]
        return pl.pallas_call(
            body,
            name=name,
            in_specs=list(specs),
            out_specs=tuple(out_specs or [VM for _ in outs]),
            out_shape=tuple(
                pltpu.HBM(s, d) if out_specs and out_specs[n] is ANY else jax.ShapeDtypeStruct(s, d)
                for n, (s, d) in enumerate(outs)
            ),
            scratch_shapes=list(scratch) + buffers + sems,
            compiler_params=pltpu.CompilerParams(vmem_limit_bytes=mib << 20),
        )(*args)

    return build


def swap(value, axis, count, mask):
    return lax.ppermute(value, axis, [(i, i ^ mask) for i in range(count)])


def local(
    x_in,
    w_inner,
    w_bc,
    w_dt,
    conv_x_w,
    conv_bc_w,
    dt_bias,
    a_log,
    d_skip,
    norm_gain,
    w_out,
    ssm_state,
    conv_x_state,
    conv_bc_state,
    parents,
):
    beam = lax.axis_index("beam")
    d_local = x_in.shape[-1]
    heads = ssm_state.shape[2]
    parent_column = parents.reshape(STEPS, 8, 4).transpose(2, 1, 0).reshape(ROWS, 1)
    x = x_in.reshape(ROWS, d_local)

    inner = jnp.einsum("rd,dzk->rzk", x, w_inner, preferred_element_type=F32).astype(BF16)
    inner = inner[:, ::-1].reshape(ROWS, 2, heads, HD).transpose(2, 0, 1, 3).reshape(heads, ROWS, 2 * HD)
    bc = jnp.einsum("rd,dzk->rzk", x, w_bc, preferred_element_type=F32).astype(BF16).reshape(ROWS, 128)
    top = jnp.concatenate([inner, jnp.broadcast_to(bc[None], (heads, ROWS, 128))], axis=2)
    dt = jnp.einsum("dh,rd->hr", w_dt, x, preferred_element_type=F32)
    dt_high = lax.reduce_precision(dt, 8, 7)
    dt_row = jnp.concatenate([dt_high, dt - dt_high], axis=1).astype(BF16)[:, None]
    taps_x = conv_x_state.transpose(2, 4, 0, 1, 3).reshape(heads, 12, HD)
    taps_bc = jnp.broadcast_to(conv_bc_state.transpose(2, 0, 1, 3, 4).reshape(1, 12, 128), (heads, 12, 128))
    extra = jnp.concatenate([taps_x, jnp.zeros((heads, 12, HD), BF16), taps_bc], axis=2)
    bottom = jnp.concatenate([extra, dt_row, jnp.zeros((heads, 3, 256), BF16)], axis=1)
    payload = jnp.concatenate([top, bottom], axis=1)
    recv = lax.all_to_all(payload, "beam", split_axis=0, concat_axis=0, tiled=True)

    packed = call(
        pack_kernel,
        "pack",
        [ANY],
        [((4, HD, NS), BF16)] * 8,
        [pltpu.SemaphoreType.DMA((8, 4))],
    )(ssm_state)
    states = [packed[0]] + [swap(packed[k], "beam", 8, k) for k in range(1, 8)]

    new, conv, bc_conv, dt_raw, fin = call(
        conv_kernel,
        "conv",
        [FAR, VM, VM, VM],
        [((ROWS, 256), BF16), ((ROWS, 128), BF16), ((ROWS, 128), BF16), ((1, ROWS), F32), ((3, BEAMS, 256), BF16)],
        [pltpu.VMEM((3, BEAMS, 256), F32)],
    )(recv, parent_column, conv_x_w, conv_bc_w.reshape(4, 128))

    others = [swap(bc_conv, "row", 32, k) for k in (1, 2, 3)]

    send, b_in, coef, first = call(
        scan_kernel,
        "scan",
        [VM] * 12 + [ANY] * 8,
        [((8, ROWS, 128), BF16), ((ROWS, NS), BF16), ((ROWS, ROWS), F32), ((ROWS, 128), F32)],
        [
            pltpu.VMEM((BEAMS, HD, NS), BF16),
            pltpu.VMEM((ROWS, 128), BF16),
            pltpu.VMEM((ROWS, NS), BF16),
            pltpu.VMEM((ROWS, ROWS), F32),
            pltpu.VMEM((ROWS, 128), F32),
            pltpu.SemaphoreType.DMA((8,)),
            pltpu.SemaphoreType.DMA((11,)),
        ],
        out_specs=[ANY] * 4,
    )(
        parent_column,
        new,
        conv,
        bc_conv,
        *others,
        dt_raw,
        norm_gain.reshape(1, 512),
        a_log.reshape(1, 8),
        dt_bias.reshape(1, 8),
        d_skip.reshape(1, 8),
        *states,
    )
    gathered = lax.all_to_all(send, "beam", split_axis=0, concat_axis=0, tiled=True)
    final = list(call(
        final_kernel,
        "final",
        [SM, VM] + [FAR] * 4 + [ANY] * 8,
        [((4 * HD + 16, NS), BF16)] * 8,
        [
            pltpu.VMEM((BEAMS, HD, NS), BF16),
            pltpu.VMEM((8, 4 * HD + 16, NS), BF16),
            pltpu.SemaphoreType.DMA((8,)),
            pltpu.SemaphoreType.DMA((8,)),
        ],
        out_specs=[ANY] * 8,
    )(parents.reshape(ROWS), conv, b_in, coef, first, fin, *states))
    homes = [final[0]] + [swap(final[k], "beam", 8, k) for k in range(1, 8)]
    (parts,) = call(
        out_kernel,
        "project",
        [VM, VM],
        [((BEAMS, STEPS, 1152), BF16)],
    )(gathered, w_out)
    parts, homes[1], homes[2], homes[6] = lax.optimization_barrier((parts, homes[1], homes[2], homes[6]))
    spread = lax.all_to_all(parts, "row", split_axis=0, concat_axis=0, tiled=True)
    ssm_final, conv_x_rows = call(
        unpack_kernel,
        "unpack",
        [VM] * 8,
        [((SESS, 2, heads, HD, NS), BF16), ((SESS, 2, 3, heads, HD), BF16)],
        [
            pltpu.VMEM((8, 16, NS), F32),
            pltpu.SemaphoreType.DMA((8, 4)),
        ],
        out_specs=[ANY, VM],
    )(*homes)
    conv_x_final = conv_x_rows.transpose(0, 1, 3, 4, 2)

    (layer_out,) = call(norm_kernel, "norm", [VM], [((STEPS, 1024), BF16)])(spread)
    layer_out = layer_out[:, None]

    own = lax.dynamic_slice_in_dim(fin, beam * 4, 4, 1)[:, :, 128:]
    conv_bc_final = own.reshape(3, SESS, 2, 2, 64).transpose(1, 2, 0, 3, 4)
    return layer_out, ssm_final, conv_x_final, conv_bc_final


def solution(mesh):
    placed = (
        P(None, None, None, "beam"),
        P("beam", None, "row"),
        P("beam", None, "row"),
        P("beam", "row"),
        P(None, "row"),
        P(None, None, "row"),
        P("row"),
        P("row"),
        P("row"),
        P("row"),
        P("row", "beam"),
        P(None, "beam", "row", None, None),
        P(None, "beam", "row", None, None),
        P(None, "beam", None, None, "row"),
        P(),
    )
    return jax.shard_map(
        local,
        mesh=mesh,
        in_specs=placed,
        out_specs=(
            P(None, "row", "beam"),
            P(None, "beam", "row", None, None),
            P(None, "beam", "row", None, None),
            P(None, "beam", None, None, "row"),
        ),
        check_vma=False,
    )
```

```python
import jax
import jax.numpy as jnp
from jax import lax
from jax.experimental import pallas as pl
from jax.experimental.pallas import tpu as pltpu
from jax.sharding import PartitionSpec as P

EPS = 1e-05
F32 = jnp.float32
BF16 = jnp.bfloat16
STEPS = 4
SESS = 2
WIDTH = 16
BEAMS = SESS * WIDTH
ROWS = STEPS * BEAMS
HD = 64
NS = 256
GROUP_CH = 2048.0


def row_of(step, s, b):
    v = s * WIDTH + b
    return (v % 4) * 32 + (v // 4) * 4 + step


def dot(a, b):
    return jnp.dot(a, b, preferred_element_type=F32)


def dot_t(a, b):
    return lax.dot_general(a, b, (((1,), (1,)), ((), ())), preferred_element_type=F32)


def lineage(par):
    r = lax.broadcasted_iota(jnp.int32, (ROWS, 1), 0)
    t = r & 3
    s = (r & 31) >> 4
    before = (par & 3) * 32 + (s * 4 + (par >> 2)) * 4 + t - 1
    before = jnp.where(t > 0, before, -1)
    start = jnp.where(t == 0, (par >> 1) * 4 + s * 2 + (par & 1), -1)
    lanes = lax.broadcasted_iota(jnp.int32, (ROWS, ROWS), 1)
    a1 = jnp.where(lanes == before, 1.0, 0.0)
    lanes_i = lax.broadcasted_iota(jnp.int32, (ROWS, BEAMS), 1)
    g = jnp.where(lanes_i == start, 1.0, 0.0)
    a1b = a1.astype(BF16)
    a2 = dot(a1b, a1b)
    a3 = dot(a1b, a2.astype(BF16))
    gb = g.astype(BF16)
    g1 = dot(a1b, gb)
    g2 = dot(a1b, g1.astype(BF16))
    g3 = dot(a1b, g2.astype(BF16))
    return t, a1, a2, a3, g + g1 + g2 + g3


def head_part(ref, width):
    head = lax.axis_index("beam")
    part = jnp.zeros((ref.shape[0], width), F32)
    for h in range(8):
        part = part + jnp.where(head == h, ref[:, width * h : width * h + width].astype(F32), 0.0)
    return part


def head_value(ref):
    lane = lax.broadcasted_iota(jnp.int32, (1, 8), 1)
    return jnp.sum(jnp.where(lane == lax.axis_index("beam"), ref[...], 0.0), axis=1, keepdims=True)


def pack_kernel(state, *refs):
    outs, (held, sem_in, sem_out) = refs[:4], refs[4:]
    head = lax.axis_index("beam")
    loads = []
    for k in range(8):
        for j in range(4):
            loads.append(
                pltpu.make_async_copy(state.at[j // 2, j % 2, head ^ k], held.at[k // 2, k % 2, j], sem_in.at[k, j])
            )
            loads[-1].start()
    copies = []
    for c in range(4):
        for load in loads[8 * c : 8 * c + 8]:
            load.wait()
        copies.append(pltpu.make_async_copy(held.at[c], outs[c], sem_out.at[c]))
        copies[-1].start()
    for copy in copies:
        copy.wait()


def merge_kernel(p0, p1, p2, p3, out, held, sems):
    loads = [pltpu.make_async_copy(p.at[1], held.at[c], sems.at[c]) for c, p in enumerate((p0, p1, p2, p3))]
    for load in loads:
        load.start()
    for load in loads:
        load.wait()
    copy = pltpu.make_async_copy(held, out, sems.at[4])
    copy.start()
    copy.wait()


def arrived(parts):
    return [(k, parts[4].at[k // 2] if k % 2 else parts[k // 2].at[0]) for k in range(8)]


def conv_kernel(recv, par, conv_x_w, conv_bc_w, sum_out, conv_out, bc_out, dt_out, fin_out, init):
    total = recv[0, 0:ROWS, :].astype(F32)
    dt = recv[0, 128:144, :].astype(F32)
    for k in range(3):
        init[k, 0:4, :] = dt[4 * k : 4 * k + 4]
    for i in range(1, 8):
        total = total + recv[i, 0:ROWS, :].astype(F32)
        extra = recv[i, 128:144, :].astype(F32)
        for k in range(3):
            init[k, 4 * i : 4 * i + 4, :] = extra[4 * k : 4 * k + 4]
        dt = dt + extra
    dt_out[...] = dt[12:13, 0:128] + dt[12:13, 128:256]
    new = total.astype(BF16)
    t, a1, a2, a3, g = lineage(par[...])
    gb = g.astype(BF16)
    start = [dot(gb, init[k].astype(BF16)) for k in range(3)]
    past1 = dot(a1.astype(BF16), new) + jnp.where(t == 0, start[2], 0.0)
    past2 = dot(a2.astype(BF16), new) + jnp.where(t == 0, start[1], 0.0) + jnp.where(t == 1, start[2], 0.0)
    past3 = (
        dot(a3.astype(BF16), new)
        + jnp.where(t == 0, start[0], 0.0)
        + jnp.where(t == 1, start[1], 0.0)
        + jnp.where(t == 2, start[2], 0.0)
    )
    w = jnp.concatenate([head_part(conv_x_w, HD), jnp.zeros((4, HD), F32), conv_bc_w[...].astype(F32)], axis=1)
    mixed = w[0:1] * past3 + w[1:2] * past2 + w[2:3] * past1 + w[3:4] * new.astype(F32)
    conv = mixed / (1.0 + jnp.exp(-mixed))
    sum_out[...] = new
    conv_out[...] = conv[:, 0:128].astype(BF16)
    bc_out[...] = conv[:, 128:256].astype(BF16)
    e = lax.broadcasted_iota(jnp.int32, (BEAMS, ROWS), 0)
    b = (e >> 2) * 2 + (e & 1)
    s = (e >> 1) & 1
    last = (b & 3) * 32 + (s * 4 + (b >> 2)) * 4 + STEPS - 1
    pick = jnp.where(lax.broadcasted_iota(jnp.int32, (BEAMS, ROWS), 1) == last, 1.0, 0.0).astype(BF16)
    fin_out[0] = dot(pick, past2.astype(BF16)).astype(BF16)
    fin_out[1] = dot(pick, past1.astype(BF16)).astype(BF16)
    fin_out[2] = dot(pick, new).astype(BF16)


def group_columns(blocks, low):
    b_cols, c_cols = [], []
    for q in range(4):
        part = jnp.zeros((ROWS, 128), F32)
        for k in range(4):
            part = part + jnp.where(low == (q ^ k), blocks[k], 0.0)
        b_cols.append(part[:, 0:64])
        c_cols.append(part[:, 64:128])
    return jnp.concatenate(b_cols, 1).astype(BF16), jnp.concatenate(c_cols, 1).astype(BF16)


def scan_kernel(
    par, new, conv, bc0, bc1, bc2, bc3, dt_raw, norm_gain, a_log, dt_bias, d_skip, *refs
):
    parts, (send_out, b_out, coef_out, first_out) = refs[:5], refs[5:9]
    state, send, b_buf, coef_buf, first_buf, sem_in, sem_send = refs[9:]
    head = lax.axis_index("beam")
    loads = [pltpu.make_async_copy(p, state.at[pl.ds((head ^ k) * 4, 4)], sem_in.at[k]) for k, p in arrived(parts)]
    for load in loads:
        load.start()
    low = lax.axis_index("row") & 3
    blocks = [ref[...].astype(F32) for ref in (bc0, bc1, bc2, bc3)]
    b_in, c_out = group_columns(blocks, low)
    t, a1, a2, a3, g = lineage(par[...])
    raw = dt_raw[...].astype(BF16).astype(F32) + head_value(dt_bias)
    step_size = jnp.maximum(raw, 0.0) + jnp.log1p(jnp.exp(-jnp.abs(raw)))
    rate = jnp.exp(head_value(a_log))
    log_decay = -rate * step_size
    rr = lax.broadcasted_iota(jnp.int32, (ROWS, ROWS), 0)
    cc = lax.broadcasted_iota(jnp.int32, (ROWS, ROWS), 1)
    eye = jnp.where(rr == cc, 1.0, 0.0)
    path1 = jnp.sum(eye * log_decay, axis=1, keepdims=True)
    path2 = path1 + jnp.sum(a1 * log_decay, axis=1, keepdims=True)
    path3 = path2 + jnp.sum(a2 * log_decay, axis=1, keepdims=True)
    path4 = path3 + jnp.sum(a3 * log_decay, axis=1, keepdims=True)
    coef = (eye + a1 * jnp.exp(path1) + a2 * jnp.exp(path2) + a3 * jnp.exp(path3)) * step_size
    first = jnp.exp(path4)
    x_conv = conv[:, 0:64]
    inner = dot_t(c_out, b_in) * coef
    read = jnp.dot(inner, x_conv.astype(F32), precision=lax.Precision.HIGHEST, preferred_element_type=F32)
    lanes_i = lax.broadcasted_iota(jnp.int32, (ROWS, BEAMS), 1).astype(F32)
    origin = jnp.sum(g * lanes_i, axis=1, keepdims=True)
    half = jnp.where(lax.broadcasted_iota(jnp.int32, (ROWS, 128), 1) < 64, 0.0, 1.0)
    origin_b = jnp.broadcast_to(origin, (ROWS, 128)) - half
    acc = jnp.zeros((ROWS, 128), F32)
    for load in loads:
        load.wait()
    for p in range(BEAMS // 2):
        both = state[2 * p : 2 * p + 2].reshape(2 * HD, NS)
        acc = acc + jnp.where(origin_b == float(2 * p), dot_t(c_out, both), 0.0)
    old = acc[:, 0:64] + acc[:, 64:128]
    x_val = x_conv.astype(F32)
    read = read + first * old + head_value(d_skip) * x_val
    gate = new[:, 64:128].astype(F32)
    gated = read * (gate / (1.0 + jnp.exp(-gate)))
    square = jnp.sum(gated * gated, axis=1, keepdims=True)
    high = square.astype(BF16).astype(F32)
    rest = square - high
    lane = lax.broadcasted_iota(jnp.int32, (ROWS, 64), 1)
    stats = jnp.where(lane == 0, high, jnp.where(lane == 1, rest, 0.0))
    send[...] = jnp.concatenate([gated * head_part(norm_gain, HD), stats], axis=1).astype(BF16)
    sends = [pltpu.make_async_copy(send, send_out.at[k], sem_send.at[k]) for k in range(8)]
    for copy in sends:
        copy.start()
    b_buf[...] = b_in
    coef_buf[...] = coef
    first_buf[...] = jnp.broadcast_to(first, (ROWS, 128))
    for n, (buf, ref) in enumerate(((b_buf, b_out), (coef_buf, coef_out), (first_buf, first_out))):
        sends.append(pltpu.make_async_copy(buf, ref, sem_send.at[8 + n]))
        sends[-1].start()
    for copy in sends:
        copy.wait()


def final_kernel(parents, conv, b_in, coef_ref, first_ref, fin, *refs):
    parts, homes = refs[:5], refs[5:9]
    state, block, sem_in, sem_home = refs[9:]
    head = lax.axis_index("beam")
    loads = [pltpu.make_async_copy(p, state.at[pl.ds((head ^ k) * 4, 4)], sem_in.at[k]) for k, p in arrived(parts)]
    for load in loads:
        load.start()
    x_t = conv[...].astype(F32).T[0:HD]
    b = b_in[...]
    for load in loads:
        load.wait()
    saves = []
    for i in range(8):
        rows = [row_of(STEPS - 1, j // 2, 2 * i + j % 2) for j in range(4)]
        left = jnp.concatenate([x_t * coef_ref[row : row + 1, :] for row in rows], axis=0).astype(BF16)
        update = dot(left, b)
        for j in range(4):
            s, at = j // 2, 2 * i + j % 2
            for step in range(STEPS - 1, -1, -1):
                at = parents[step * BEAMS + s * WIDTH + at]
            origin = (at >> 1) * 4 + s * 2 + (at & 1)
            keep = jnp.broadcast_to(first_ref[rows[j] : rows[j] + 1, 0:1], (HD, NS))
            value = keep * state[origin].astype(F32) + update[HD * j : HD * j + HD]
            block[i, HD * j : HD * j + HD, :] = value.astype(BF16)
        taps = [fin[k, 4 * i : 4 * i + 4, 0:64].astype(F32) for k in range(3)]
        tail = jnp.concatenate(taps + [jnp.zeros((4, 64), F32)], axis=1)
        block[i, 4 * HD : 4 * HD + 16, :] = jnp.concatenate([tail, jnp.zeros((12, NS), F32)], axis=0).astype(BF16)
    for k in range(8):
        saves.append(pltpu.make_async_copy(block.at[head ^ k], homes[k // 2].at[k % 2], sem_home.at[k]))
        saves[-1].start()
    for copy in saves:
        copy.wait()


def unpack_kernel(*refs):
    parts, (ssm_out, conv_out), (held, sem_in, sem_out) = refs[:5], refs[5:7], refs[7:]
    head = lax.axis_index("beam")
    loads = [pltpu.make_async_copy(p, held.at[head ^ k], sem_in.at[k]) for k, p in arrived(parts)]
    for load in loads:
        load.start()
    copies = []
    for k in range(8):
        loads[k].wait()
        h = head ^ k
        for j in range(4):
            src = held.at[h, pl.ds(HD * j, HD)]
            copies.append(pltpu.make_async_copy(src, ssm_out.at[j // 2, j % 2, h], sem_out.at[k, j]))
            copies[-1].start()
    for h in range(8):
        tail = held[h, 4 * HD : 4 * HD + 16, :].astype(F32)
        for j in range(4):
            for k in range(3):
                conv_out[j // 2, j % 2, k, h : h + 1, :] = tail[j : j + 1, HD * k : HD * k + HD].astype(BF16)
    for copy in copies:
        copy.wait()


def out_kernel(recv, w_out, out):
    stats = recv[0, :, 64:128].astype(F32)
    for i in range(1, 8):
        stats = stats + recv[i, :, 64:128].astype(F32)
    square = stats[:, 0:1] + stats[:, 1:2]
    high = square.astype(BF16).astype(F32)
    rest = square - high
    lane = lax.broadcasted_iota(jnp.int32, (ROWS, 128), 1)
    tail = jnp.where(lane == 0, high, jnp.where(lane == 1, rest, 0.0))
    left = jnp.concatenate([recv[i, :, 0:64] for i in range(8)], axis=1)
    full = jnp.concatenate([dot(left, w_out[...]), tail], axis=1)
    for q in range(4):
        for m in range(8):
            out[4 * m + q] = full[32 * q + 4 * m : 32 * q + 4 * m + 4].astype(BF16)


def norm_kernel(recv, out):
    result = jnp.zeros((STEPS, 1024), F32)
    for g in range(8):
        total = recv[4 * g].astype(F32)
        for j in range(1, 4):
            total = total + recv[4 * g + j].astype(F32)
        square = total[:, 1024:1025] + total[:, 1025:1026]
        result = result + total[:, 0:1024] * lax.rsqrt(square * (1.0 / GROUP_CH) + EPS)
    out[...] = result.astype(BF16)


VM = pl.BlockSpec(memory_space=pltpu.VMEM)
SM = pl.BlockSpec(memory_space=pltpu.SMEM)
ANY = pl.BlockSpec(memory_space=pl.ANY)
FAR = pl.BlockSpec(memory_space=pltpu.HBM)


def call(kernel, name, specs, outs, scratch=(), mib=6, out_specs=None):
    def build(*args):
        far = [n for n, spec in enumerate(specs) if spec is FAR]
        count = len(specs)
        buffers = [pltpu.VMEM(args[n].shape, args[n].dtype) for n in far]
        sems = [pltpu.SemaphoreType.DMA((len(far),))] if far else []

        def body(*refs):
            ins = list(refs[:count])
            rest = refs[count : count + len(outs) + len(scratch)]
            held = refs[count + len(outs) + len(scratch) :]
            copies = [pltpu.make_async_copy(ins[n], held[k], held[-1].at[k]) for k, n in enumerate(far)]
            for copy in copies:
                copy.start()
            for copy in copies:
                copy.wait()
            for k, n in enumerate(far):
                ins[n] = held[k]
            kernel(*ins, *rest)

        args = [
            pltpu.with_memory_space_constraint(arg, pltpu.HBM) if specs[n] in (ANY, FAR) else arg
            for n, arg in enumerate(args)
        ]
        return pl.pallas_call(
            body,
            name=name,
            in_specs=list(specs),
            out_specs=tuple(out_specs or [VM for _ in outs]),
            out_shape=tuple(
                pltpu.HBM(s, d) if out_specs and out_specs[n] is ANY else jax.ShapeDtypeStruct(s, d)
                for n, (s, d) in enumerate(outs)
            ),
            scratch_shapes=list(scratch) + buffers + sems,
            compiler_params=pltpu.CompilerParams(vmem_limit_bytes=mib << 20),
        )(*args)

    return build


def swap(value, axis, count, mask):
    return lax.ppermute(value, axis, [(i, i ^ mask) for i in range(count)])


def chips(blocks):
    return [blocks[0]] + [swap(blocks[c], "beam", 8, 2 * c) for c in range(1, 4)]


def cores(got, name):
    shape = (4,) + got[0].shape[1:]
    (merged,) = call(
        merge_kernel,
        name,
        [ANY] * 4,
        [(shape, BF16)],
        [pltpu.VMEM(shape, BF16), pltpu.SemaphoreType.DMA((5,))],
        out_specs=[ANY],
    )(*got)
    return got + [swap(merged, "beam", 8, 1)]


def local(
    x_in,
    w_inner,
    w_bc,
    w_dt,
    conv_x_w,
    conv_bc_w,
    dt_bias,
    a_log,
    d_skip,
    norm_gain,
    w_out,
    ssm_state,
    conv_x_state,
    conv_bc_state,
    parents,
):
    beam = lax.axis_index("beam")
    d_local = x_in.shape[-1]
    heads = ssm_state.shape[2]
    parent_column = parents.reshape(STEPS, 8, 4).transpose(2, 1, 0).reshape(ROWS, 1)
    x = x_in.reshape(STEPS, 8, 4, d_local).transpose(2, 1, 0, 3).reshape(ROWS, d_local)

    inner = jnp.einsum("rd,dzk->rzk", x, w_inner, preferred_element_type=F32).astype(BF16)
    inner = inner[:, ::-1].reshape(ROWS, 2, heads, HD).transpose(2, 0, 1, 3).reshape(heads, ROWS, 2 * HD)
    bc = jnp.einsum("rd,dzk->rzk", x, w_bc, preferred_element_type=F32).astype(BF16).reshape(ROWS, 128)
    top = jnp.concatenate([inner, jnp.broadcast_to(bc[None], (heads, ROWS, 128))], axis=2)
    dt = jnp.einsum("dh,rd->hr", w_dt, x, preferred_element_type=F32)
    dt_high = lax.reduce_precision(dt, 8, 7)
    dt_row = jnp.concatenate([dt_high, dt - dt_high], axis=1).astype(BF16)[:, None]
    taps_x = conv_x_state.transpose(2, 4, 0, 1, 3).reshape(heads, 12, HD)
    taps_bc = jnp.broadcast_to(conv_bc_state.transpose(2, 0, 1, 3, 4).reshape(1, 12, 128), (heads, 12, 128))
    extra = jnp.concatenate([taps_x, jnp.zeros((heads, 12, HD), BF16), taps_bc], axis=2)
    bottom = jnp.concatenate([extra, dt_row, jnp.zeros((heads, 3, 256), BF16)], axis=1)
    payload = jnp.concatenate([top, bottom], axis=1)
    recv = lax.all_to_all(payload, "beam", split_axis=0, concat_axis=0, tiled=True)

    packed = call(
        pack_kernel,
        "pack",
        [ANY],
        [((2, 4, HD, NS), BF16)] * 4,
        [
            pltpu.VMEM((4, 2, 4, HD, NS), BF16),
            pltpu.SemaphoreType.DMA((8, 4)),
            pltpu.SemaphoreType.DMA((4,)),
        ],
        out_specs=[ANY] * 4,
    )(ssm_state)
    halves = chips(packed)

    new, conv, bc_conv, dt_raw, fin = call(
        conv_kernel,
        "conv",
        [FAR, VM, VM, VM],
        [((ROWS, 256), BF16), ((ROWS, 128), BF16), ((ROWS, 128), BF16), ((1, ROWS), F32), ((3, BEAMS, 256), BF16)],
        [pltpu.VMEM((3, BEAMS, 256), F32)],
    )(recv, parent_column, conv_x_w, conv_bc_w.reshape(4, 128))

    _, *halves = lax.optimization_barrier((bc_conv, *halves))
    states = cores(halves, "states")
    others = [swap(bc_conv, "row", 32, k) for k in (1, 2, 3)]

    send, b_in, coef, first = call(
        scan_kernel,
        "scan",
        [VM] * 12 + [ANY] * 5,
        [((8, ROWS, 128), BF16), ((ROWS, NS), BF16), ((ROWS, ROWS), F32), ((ROWS, 128), F32)],
        [
            pltpu.VMEM((BEAMS, HD, NS), BF16),
            pltpu.VMEM((ROWS, 128), BF16),
            pltpu.VMEM((ROWS, NS), BF16),
            pltpu.VMEM((ROWS, ROWS), F32),
            pltpu.VMEM((ROWS, 128), F32),
            pltpu.SemaphoreType.DMA((8,)),
            pltpu.SemaphoreType.DMA((11,)),
        ],
        out_specs=[ANY] * 4,
    )(
        parent_column,
        new,
        conv,
        bc_conv,
        *others,
        dt_raw,
        norm_gain.reshape(1, 512),
        a_log.reshape(1, 8),
        dt_bias.reshape(1, 8),
        d_skip.reshape(1, 8),
        *states,
    )
    gathered = lax.all_to_all(send, "beam", split_axis=0, concat_axis=0, tiled=True)
    final = list(call(
        final_kernel,
        "final",
        [SM, VM] + [FAR] * 4 + [ANY] * 5,
        [((2, 4 * HD + 16, NS), BF16)] * 4,
        [
            pltpu.VMEM((BEAMS, HD, NS), BF16),
            pltpu.VMEM((8, 4 * HD + 16, NS), BF16),
            pltpu.SemaphoreType.DMA((8,)),
            pltpu.SemaphoreType.DMA((8,)),
        ],
        out_specs=[ANY] * 4,
    )(parents.reshape(ROWS), conv, b_in, coef, first, fin, *states))
    gathered, *final = lax.optimization_barrier((gathered, *final))
    homes = cores(chips(final), "finals")
    (parts,) = call(
        out_kernel,
        "project",
        [VM, VM],
        [((BEAMS, STEPS, 1152), BF16)],
    )(gathered, w_out)
    spread = lax.all_to_all(parts, "row", split_axis=0, concat_axis=0, tiled=True)
    ssm_final, conv_x_rows = call(
        unpack_kernel,
        "unpack",
        [ANY] * 5,
        [((SESS, 2, heads, HD, NS), BF16), ((SESS, 2, 3, heads, HD), BF16)],
        [
            pltpu.VMEM((8, 4 * HD + 16, NS), BF16),
            pltpu.SemaphoreType.DMA((8,)),
            pltpu.SemaphoreType.DMA((8, 4)),
        ],
        out_specs=[ANY, VM],
    )(*homes)
    spread, conv_x_rows = lax.optimization_barrier((spread, conv_x_rows))
    (layer_out,) = call(norm_kernel, "norm", [VM], [((STEPS, 1024), BF16)])(spread)
    layer_out = layer_out[:, None]
    conv_x_final = conv_x_rows.transpose(0, 1, 3, 4, 2)

    own = lax.dynamic_slice_in_dim(fin, beam * 4, 4, 1)[:, :, 128:]
    conv_bc_final = own.reshape(3, SESS, 2, 2, 64).transpose(1, 2, 0, 3, 4)
    return layer_out, ssm_final, conv_x_final, conv_bc_final


def solution(mesh):
    placed = (
        P(None, None, None, "beam"),
        P("beam", None, "row"),
        P("beam", None, "row"),
        P("beam", "row"),
        P(None, "row"),
        P(None, None, "row"),
        P("row"),
        P("row"),
        P("row"),
        P("row"),
        P("row", "beam"),
        P(None, "beam", "row", None, None),
        P(None, "beam", "row", None, None),
        P(None, "beam", None, None, "row"),
        P(),
    )
    return jax.shard_map(
        local,
        mesh=mesh,
        in_specs=placed,
        out_specs=(
            P(None, "row", "beam"),
            P(None, "beam", "row", None, None),
            P(None, "beam", "row", None, None),
            P(None, "beam", None, None, "row"),
        ),
        check_vma=False,
    )
```

```python
import jax
import jax.numpy as jnp
from jax import lax
from jax.experimental import pallas as pl
from jax.experimental.pallas import tpu as pltpu
from jax.sharding import PartitionSpec as P

EPS = 1e-05
F32 = jnp.float32
BF16 = jnp.bfloat16
STEPS = 4
SESS = 2
WIDTH = 16
BEAMS = SESS * WIDTH
ROWS = STEPS * BEAMS
HD = 64
NS = 256
GROUP_CH = 2048.0


def row_of(step, s, b):
    v = s * WIDTH + b
    return (v % 4) * 32 + (v // 4) * 4 + step


def dot(a, b):
    return jnp.dot(a, b, preferred_element_type=F32)


def dot_t(a, b):
    return lax.dot_general(a, b, (((1,), (1,)), ((), ())), preferred_element_type=F32)


def lineage(par):
    r = lax.broadcasted_iota(jnp.int32, (ROWS, 1), 0)
    t = r & 3
    s = (r & 31) >> 4
    before = (par & 3) * 32 + (s * 4 + (par >> 2)) * 4 + t - 1
    before = jnp.where(t > 0, before, -1)
    start = jnp.where(t == 0, (par >> 1) * 4 + s * 2 + (par & 1), -1)
    lanes = lax.broadcasted_iota(jnp.int32, (ROWS, ROWS), 1)
    a1 = jnp.where(lanes == before, 1.0, 0.0)
    lanes_i = lax.broadcasted_iota(jnp.int32, (ROWS, BEAMS), 1)
    g = jnp.where(lanes_i == start, 1.0, 0.0)
    a1b = a1.astype(BF16)
    a2 = dot(a1b, a1b)
    a3 = dot(a1b, a2.astype(BF16))
    gb = g.astype(BF16)
    g1 = dot(a1b, gb)
    g2 = dot(a1b, g1.astype(BF16))
    g3 = dot(a1b, g2.astype(BF16))
    return t, a1, a2, a3, g + g1 + g2 + g3


def head_part(ref, width):
    head = lax.axis_index("beam")
    part = jnp.zeros((ref.shape[0], width), F32)
    for h in range(8):
        part = part + jnp.where(head == h, ref[:, width * h : width * h + width].astype(F32), 0.0)
    return part


def head_value(ref):
    lane = lax.broadcasted_iota(jnp.int32, (1, 8), 1)
    return jnp.sum(jnp.where(lane == lax.axis_index("beam"), ref[...], 0.0), axis=1, keepdims=True)


def pack_kernel(state, *refs):
    outs, (held, sem_in, sem_out) = refs[:4], refs[4:]
    head = lax.axis_index("beam")
    loads = []
    for k in range(8):
        for j in range(4):
            loads.append(
                pltpu.make_async_copy(state.at[j // 2, j % 2, head ^ k], held.at[k // 2, k % 2, j], sem_in.at[k, j])
            )
            loads[-1].start()
    copies = []
    for c in range(4):
        for load in loads[8 * c : 8 * c + 8]:
            load.wait()
        copies.append(pltpu.make_async_copy(held.at[c], outs[c], sem_out.at[c]))
        copies[-1].start()
    for copy in copies:
        copy.wait()


def merge_kernel(p0, p1, p2, p3, out, held, sems):
    loads = [pltpu.make_async_copy(p.at[1], held.at[c], sems.at[c]) for c, p in enumerate((p0, p1, p2, p3))]
    for load in loads:
        load.start()
    for load in loads:
        load.wait()
    copy = pltpu.make_async_copy(held, out, sems.at[4])
    copy.start()
    copy.wait()


def arrived(parts):
    return [(k, parts[4].at[k // 2] if k % 2 else parts[k // 2].at[0]) for k in range(8)]


def conv_kernel(recv, par, conv_x_w, conv_bc_w, sum_out, conv_out, bc_out, dt_out, fin_out, init):
    total = recv[0, 0:ROWS, :].astype(F32)
    dt = recv[0, 128:144, :].astype(F32)
    for k in range(3):
        init[k, 0:4, :] = dt[4 * k : 4 * k + 4]
    for i in range(1, 8):
        total = total + recv[i, 0:ROWS, :].astype(F32)
        extra = recv[i, 128:144, :].astype(F32)
        for k in range(3):
            init[k, 4 * i : 4 * i + 4, :] = extra[4 * k : 4 * k + 4]
        dt = dt + extra
    dt_out[...] = dt[12:13, 0:128] + dt[12:13, 128:256]
    new = total.astype(BF16)
    t, a1, a2, a3, g = lineage(par[...])
    gb = g.astype(BF16)
    start = [dot(gb, init[k].astype(BF16)) for k in range(3)]
    past1 = dot(a1.astype(BF16), new) + jnp.where(t == 0, start[2], 0.0)
    past2 = dot(a2.astype(BF16), new) + jnp.where(t == 0, start[1], 0.0) + jnp.where(t == 1, start[2], 0.0)
    past3 = (
        dot(a3.astype(BF16), new)
        + jnp.where(t == 0, start[0], 0.0)
        + jnp.where(t == 1, start[1], 0.0)
        + jnp.where(t == 2, start[2], 0.0)
    )
    w = jnp.concatenate([head_part(conv_x_w, HD), jnp.zeros((4, HD), F32), conv_bc_w[...].astype(F32)], axis=1)
    mixed = w[0:1] * past3 + w[1:2] * past2 + w[2:3] * past1 + w[3:4] * new.astype(F32)
    conv = mixed / (1.0 + jnp.exp(-mixed))
    sum_out[...] = new
    conv_out[...] = conv[:, 0:128].astype(BF16)
    bc_out[...] = conv[:, 128:256].astype(BF16)
    e = lax.broadcasted_iota(jnp.int32, (BEAMS, ROWS), 0)
    b = (e >> 2) * 2 + (e & 1)
    s = (e >> 1) & 1
    last = (b & 3) * 32 + (s * 4 + (b >> 2)) * 4 + STEPS - 1
    pick = jnp.where(lax.broadcasted_iota(jnp.int32, (BEAMS, ROWS), 1) == last, 1.0, 0.0).astype(BF16)
    fin_out[0] = dot(pick, past2.astype(BF16)).astype(BF16)
    fin_out[1] = dot(pick, past1.astype(BF16)).astype(BF16)
    fin_out[2] = dot(pick, new).astype(BF16)


def group_columns(blocks, low):
    b_cols, c_cols = [], []
    for q in range(4):
        part = jnp.zeros((ROWS, 128), F32)
        for k in range(4):
            part = part + jnp.where(low == (q ^ k), blocks[k], 0.0)
        b_cols.append(part[:, 0:64])
        c_cols.append(part[:, 64:128])
    return jnp.concatenate(b_cols, 1).astype(BF16), jnp.concatenate(c_cols, 1).astype(BF16)


def scan_kernel(
    par, new, conv, bc0, bc1, bc2, bc3, dt_raw, norm_gain, a_log, dt_bias, d_skip, *refs
):
    parts, (send_out, b_out, coef_out, first_out) = refs[:5], refs[5:9]
    state, send, b_buf, coef_buf, first_buf, sem_in, sem_send = refs[9:]
    head = lax.axis_index("beam")
    loads = [pltpu.make_async_copy(p, state.at[pl.ds((head ^ k) * 4, 4)], sem_in.at[k]) for k, p in arrived(parts)]
    for load in loads:
        load.start()
    low = lax.axis_index("row") & 3
    blocks = [ref[...].astype(F32) for ref in (bc0, bc1, bc2, bc3)]
    b_in, c_out = group_columns(blocks, low)
    t, a1, a2, a3, g = lineage(par[...])
    raw = dt_raw[...].astype(BF16).astype(F32) + head_value(dt_bias)
    step_size = jnp.maximum(raw, 0.0) + jnp.log1p(jnp.exp(-jnp.abs(raw)))
    rate = jnp.exp(head_value(a_log))
    log_decay = -rate * step_size
    rr = lax.broadcasted_iota(jnp.int32, (ROWS, ROWS), 0)
    cc = lax.broadcasted_iota(jnp.int32, (ROWS, ROWS), 1)
    eye = jnp.where(rr == cc, 1.0, 0.0)
    path1 = jnp.sum(eye * log_decay, axis=1, keepdims=True)
    path2 = path1 + jnp.sum(a1 * log_decay, axis=1, keepdims=True)
    path3 = path2 + jnp.sum(a2 * log_decay, axis=1, keepdims=True)
    path4 = path3 + jnp.sum(a3 * log_decay, axis=1, keepdims=True)
    coef = (eye + a1 * jnp.exp(path1) + a2 * jnp.exp(path2) + a3 * jnp.exp(path3)) * step_size
    first = jnp.exp(path4)
    x_conv = conv[:, 0:64]
    inner = dot_t(c_out, b_in) * coef
    read = jnp.dot(inner, x_conv.astype(F32), precision=lax.Precision.HIGHEST, preferred_element_type=F32)
    lanes_i = lax.broadcasted_iota(jnp.int32, (ROWS, BEAMS), 1).astype(F32)
    origin = jnp.sum(g * lanes_i, axis=1, keepdims=True)
    half = jnp.where(lax.broadcasted_iota(jnp.int32, (ROWS, 128), 1) < 64, 0.0, 1.0)
    origin_b = jnp.broadcast_to(origin, (ROWS, 128)) - half
    acc = jnp.zeros((ROWS, 128), F32)
    for load in loads:
        load.wait()
    for p in range(BEAMS // 2):
        both = state[2 * p : 2 * p + 2].reshape(2 * HD, NS)
        acc = acc + jnp.where(origin_b == float(2 * p), dot_t(c_out, both), 0.0)
    old = acc[:, 0:64] + acc[:, 64:128]
    x_val = x_conv.astype(F32)
    read = read + first * old + head_value(d_skip) * x_val
    gate = new[:, 64:128].astype(F32)
    gated = read * (gate / (1.0 + jnp.exp(-gate)))
    square = jnp.sum(gated * gated, axis=1, keepdims=True)
    high = square.astype(BF16).astype(F32)
    rest = square - high
    lane = lax.broadcasted_iota(jnp.int32, (ROWS, 64), 1)
    stats = jnp.where(lane == 0, high, jnp.where(lane == 1, rest, 0.0))
    send[...] = jnp.concatenate([gated * head_part(norm_gain, HD), stats], axis=1).astype(BF16)
    sends = [pltpu.make_async_copy(send, send_out.at[k], sem_send.at[k]) for k in range(8)]
    for copy in sends:
        copy.start()
    b_buf[...] = b_in
    coef_buf[...] = coef
    first_buf[...] = jnp.broadcast_to(first, (ROWS, 128))
    for n, (buf, ref) in enumerate(((b_buf, b_out), (coef_buf, coef_out), (first_buf, first_out))):
        sends.append(pltpu.make_async_copy(buf, ref, sem_send.at[8 + n]))
        sends[-1].start()
    for copy in sends:
        copy.wait()


def final_kernel(parents, conv, b_in, coef_ref, first_ref, fin, *refs):
    parts, homes = refs[:5], refs[5:9]
    state, block, sem_in, sem_home = refs[9:]
    head = lax.axis_index("beam")
    loads = [pltpu.make_async_copy(p, state.at[pl.ds((head ^ k) * 4, 4)], sem_in.at[k]) for k, p in arrived(parts)]
    for load in loads:
        load.start()
    x_t = conv[...].astype(F32).T[0:HD]
    b = b_in[...]
    for load in loads:
        load.wait()
    saves = []
    for i in range(8):
        rows = [row_of(STEPS - 1, j // 2, 2 * i + j % 2) for j in range(4)]
        left = jnp.concatenate([x_t * coef_ref[row : row + 1, :] for row in rows], axis=0).astype(BF16)
        update = dot(left, b)
        for j in range(4):
            s, at = j // 2, 2 * i + j % 2
            for step in range(STEPS - 1, -1, -1):
                at = parents[step * BEAMS + s * WIDTH + at]
            origin = (at >> 1) * 4 + s * 2 + (at & 1)
            keep = jnp.broadcast_to(first_ref[rows[j] : rows[j] + 1, 0:1], (HD, NS))
            value = keep * state[origin].astype(F32) + update[HD * j : HD * j + HD]
            block[i, HD * j : HD * j + HD, :] = value.astype(BF16)
        taps = [fin[k, 4 * i : 4 * i + 4, 0:64].astype(F32) for k in range(3)]
        tail = jnp.concatenate(taps + [jnp.zeros((4, 64), F32)], axis=1)
        block[i, 4 * HD : 4 * HD + 16, :] = jnp.concatenate([tail, jnp.zeros((12, NS), F32)], axis=0).astype(BF16)
    for k in range(8):
        saves.append(pltpu.make_async_copy(block.at[head ^ k], homes[k // 2].at[k % 2], sem_home.at[k]))
        saves[-1].start()
    for copy in saves:
        copy.wait()


def unpack_kernel(*refs):
    parts, (ssm_out, conv_out), (held, sem_in, sem_out) = refs[:5], refs[5:7], refs[7:]
    head = lax.axis_index("beam")
    loads = [pltpu.make_async_copy(p, held.at[head ^ k], sem_in.at[k]) for k, p in arrived(parts)]
    for load in loads:
        load.start()
    copies = []
    for k in range(8):
        loads[k].wait()
        h = head ^ k
        for j in range(4):
            src = held.at[h, pl.ds(HD * j, HD)]
            copies.append(pltpu.make_async_copy(src, ssm_out.at[j // 2, j % 2, h], sem_out.at[k, j]))
            copies[-1].start()
    for h in range(8):
        tail = held[h, 4 * HD : 4 * HD + 16, :].astype(F32)
        for j in range(4):
            for k in range(3):
                conv_out[j // 2, j % 2, k, h : h + 1, :] = tail[j : j + 1, HD * k : HD * k + HD].astype(BF16)
    for copy in copies:
        copy.wait()


def out_kernel(recv, w_out, out):
    stats = recv[0, :, 64:128].astype(F32)
    for i in range(1, 8):
        stats = stats + recv[i, :, 64:128].astype(F32)
    square = stats[:, 0:1] + stats[:, 1:2]
    high = square.astype(BF16).astype(F32)
    rest = square - high
    lane = lax.broadcasted_iota(jnp.int32, (ROWS, 128), 1)
    tail = jnp.where(lane == 0, high, jnp.where(lane == 1, rest, 0.0))
    left = jnp.concatenate([recv[i, :, 0:64] for i in range(8)], axis=1)
    full = jnp.concatenate([dot(left, w_out[...]), tail], axis=1)
    for q in range(4):
        for m in range(8):
            out[4 * m + q] = full[32 * q + 4 * m : 32 * q + 4 * m + 4].astype(BF16)


def norm_kernel(recv, out):
    result = jnp.zeros((STEPS, 1024), F32)
    for g in range(8):
        total = recv[4 * g].astype(F32)
        for j in range(1, 4):
            total = total + recv[4 * g + j].astype(F32)
        square = total[:, 1024:1025] + total[:, 1025:1026]
        result = result + total[:, 0:1024] * lax.rsqrt(square * (1.0 / GROUP_CH) + EPS)
    out[...] = result.astype(BF16)


VM = pl.BlockSpec(memory_space=pltpu.VMEM)
SM = pl.BlockSpec(memory_space=pltpu.SMEM)
ANY = pl.BlockSpec(memory_space=pl.ANY)
FAR = pl.BlockSpec(memory_space=pltpu.HBM)


def call(kernel, name, specs, outs, scratch=(), mib=6, out_specs=None):
    def build(*args):
        far = [n for n, spec in enumerate(specs) if spec is FAR]
        count = len(specs)
        buffers = [pltpu.VMEM(args[n].shape, args[n].dtype) for n in far]
        sems = [pltpu.SemaphoreType.DMA((len(far),))] if far else []

        def body(*refs):
            ins = list(refs[:count])
            rest = refs[count : count + len(outs) + len(scratch)]
            held = refs[count + len(outs) + len(scratch) :]
            copies = [pltpu.make_async_copy(ins[n], held[k], held[-1].at[k]) for k, n in enumerate(far)]
            for copy in copies:
                copy.start()
            for copy in copies:
                copy.wait()
            for k, n in enumerate(far):
                ins[n] = held[k]
            kernel(*ins, *rest)

        args = [
            pltpu.with_memory_space_constraint(arg, pltpu.HBM) if specs[n] in (ANY, FAR) else arg
            for n, arg in enumerate(args)
        ]
        return pl.pallas_call(
            body,
            name=name,
            in_specs=list(specs),
            out_specs=tuple(out_specs or [VM for _ in outs]),
            out_shape=tuple(
                pltpu.HBM(s, d) if out_specs and out_specs[n] is ANY else jax.ShapeDtypeStruct(s, d)
                for n, (s, d) in enumerate(outs)
            ),
            scratch_shapes=list(scratch) + buffers + sems,
            compiler_params=pltpu.CompilerParams(vmem_limit_bytes=mib << 20),
        )(*args)

    return build


def swap(value, axis, count, mask):
    return lax.ppermute(value, axis, [(i, i ^ mask) for i in range(count)])


def chips(blocks):
    return [blocks[0]] + [swap(blocks[c], "beam", 8, 2 * c) for c in range(1, 4)]


def cores(got, name):
    shape = (4,) + got[0].shape[1:]
    (merged,) = call(
        merge_kernel,
        name,
        [ANY] * 4,
        [(shape, BF16)],
        [pltpu.VMEM(shape, BF16), pltpu.SemaphoreType.DMA((5,))],
        out_specs=[ANY],
    )(*got)
    return got + [swap(merged, "beam", 8, 1)]


def local(
    x_in,
    w_inner,
    w_bc,
    w_dt,
    conv_x_w,
    conv_bc_w,
    dt_bias,
    a_log,
    d_skip,
    norm_gain,
    w_out,
    ssm_state,
    conv_x_state,
    conv_bc_state,
    parents,
):
    beam = lax.axis_index("beam")
    d_local = x_in.shape[-1]
    heads = ssm_state.shape[2]
    parent_column = parents.reshape(STEPS, 8, 4).transpose(2, 1, 0).reshape(ROWS, 1)
    x = x_in.reshape(STEPS, 8, 4, d_local).transpose(2, 1, 0, 3).reshape(ROWS, d_local)

    inner = jnp.einsum("rd,dzk->rzk", x, w_inner, preferred_element_type=F32).astype(BF16)
    inner = inner[:, ::-1].reshape(ROWS, 2, heads, HD).transpose(2, 0, 1, 3).reshape(heads, ROWS, 2 * HD)
    bc = jnp.einsum("rd,dzk->rzk", x, w_bc, preferred_element_type=F32).astype(BF16).reshape(ROWS, 128)
    top = jnp.concatenate([inner, jnp.broadcast_to(bc[None], (heads, ROWS, 128))], axis=2)
    dt = jnp.einsum("dh,rd->hr", w_dt, x, preferred_element_type=F32)
    dt_high = lax.reduce_precision(dt, 8, 7)
    dt_row = jnp.concatenate([dt_high, dt - dt_high], axis=1).astype(BF16)[:, None]
    taps_x = conv_x_state.transpose(2, 4, 0, 1, 3).reshape(heads, 12, HD)
    taps_bc = jnp.broadcast_to(conv_bc_state.transpose(2, 0, 1, 3, 4).reshape(1, 12, 128), (heads, 12, 128))
    extra = jnp.concatenate([taps_x, jnp.zeros((heads, 12, HD), BF16), taps_bc], axis=2)
    bottom = jnp.concatenate([extra, dt_row, jnp.zeros((heads, 3, 256), BF16)], axis=1)
    payload = jnp.concatenate([top, bottom], axis=1)
    recv = lax.all_to_all(payload, "beam", split_axis=0, concat_axis=0, tiled=True)

    packed = call(
        pack_kernel,
        "pack",
        [ANY],
        [((2, 4, HD, NS), BF16)] * 4,
        [
            pltpu.VMEM((4, 2, 4, HD, NS), BF16),
            pltpu.SemaphoreType.DMA((8, 4)),
            pltpu.SemaphoreType.DMA((4,)),
        ],
        out_specs=[ANY] * 4,
    )(ssm_state)
    halves = chips(packed)

    new, conv, bc_conv, dt_raw, fin = call(
        conv_kernel,
        "conv",
        [VM, VM, VM, VM],
        [((ROWS, 256), BF16), ((ROWS, 128), BF16), ((ROWS, 128), BF16), ((1, ROWS), F32), ((3, BEAMS, 256), BF16)],
        [pltpu.VMEM((3, BEAMS, 256), F32)],
    )(recv, parent_column, conv_x_w, conv_bc_w.reshape(4, 128))

    others = [swap(bc_conv, "row", 32, k) for k in (1, 2, 3)]
    gated = lax.optimization_barrier((*others, *halves))
    others, halves = list(gated[:3]), list(gated[3:])
    states = cores(halves, "states")

    send, b_in, coef, first = call(
        scan_kernel,
        "scan",
        [VM] * 12 + [ANY] * 5,
        [((8, ROWS, 128), BF16), ((ROWS, NS), BF16), ((ROWS, ROWS), F32), ((ROWS, 128), F32)],
        [
            pltpu.VMEM((BEAMS, HD, NS), BF16),
            pltpu.VMEM((ROWS, 128), BF16),
            pltpu.VMEM((ROWS, NS), BF16),
            pltpu.VMEM((ROWS, ROWS), F32),
            pltpu.VMEM((ROWS, 128), F32),
            pltpu.SemaphoreType.DMA((8,)),
            pltpu.SemaphoreType.DMA((11,)),
        ],
        out_specs=[ANY] * 4,
    )(
        parent_column,
        new,
        conv,
        bc_conv,
        *others,
        dt_raw,
        norm_gain.reshape(1, 512),
        a_log.reshape(1, 8),
        dt_bias.reshape(1, 8),
        d_skip.reshape(1, 8),
        *states,
    )
    gathered = lax.all_to_all(send, "beam", split_axis=0, concat_axis=0, tiled=True)
    final = list(call(
        final_kernel,
        "final",
        [SM, VM] + [FAR] * 4 + [ANY] * 5,
        [((2, 4 * HD + 16, NS), BF16)] * 4,
        [
            pltpu.VMEM((BEAMS, HD, NS), BF16),
            pltpu.VMEM((8, 4 * HD + 16, NS), BF16),
            pltpu.SemaphoreType.DMA((8,)),
            pltpu.SemaphoreType.DMA((8,)),
        ],
        out_specs=[ANY] * 4,
    )(parents.reshape(ROWS), conv, b_in, coef, first, fin, *states))
    gathered, *final = lax.optimization_barrier((gathered, *final))
    homes = cores(chips(final), "finals")
    (parts,) = call(
        out_kernel,
        "project",
        [VM, VM],
        [((BEAMS, STEPS, 1152), BF16)],
    )(gathered, w_out)
    spread = lax.all_to_all(parts, "row", split_axis=0, concat_axis=0, tiled=True)
    ssm_final, conv_x_rows = call(
        unpack_kernel,
        "unpack",
        [ANY] * 5,
        [((SESS, 2, heads, HD, NS), BF16), ((SESS, 2, 3, heads, HD), BF16)],
        [
            pltpu.VMEM((8, 4 * HD + 16, NS), BF16),
            pltpu.SemaphoreType.DMA((8,)),
            pltpu.SemaphoreType.DMA((8, 4)),
        ],
        out_specs=[ANY, VM],
    )(*homes)
    spread, conv_x_rows = lax.optimization_barrier((spread, conv_x_rows))
    (layer_out,) = call(norm_kernel, "norm", [VM], [((STEPS, 1024), BF16)])(spread)
    layer_out = layer_out[:, None]
    conv_x_final = conv_x_rows.transpose(0, 1, 3, 4, 2)

    own = lax.dynamic_slice_in_dim(fin, beam * 4, 4, 1)[:, :, 128:]
    conv_bc_final = own.reshape(3, SESS, 2, 2, 64).transpose(1, 2, 0, 3, 4)
    return layer_out, ssm_final, conv_x_final, conv_bc_final


def solution(mesh):
    placed = (
        P(None, None, None, "beam"),
        P("beam", None, "row"),
        P("beam", None, "row"),
        P("beam", "row"),
        P(None, "row"),
        P(None, None, "row"),
        P("row"),
        P("row"),
        P("row"),
        P("row"),
        P("row", "beam"),
        P(None, "beam", "row", None, None),
        P(None, "beam", "row", None, None),
        P(None, "beam", None, None, "row"),
        P(),
    )
    return jax.shard_map(
        local,
        mesh=mesh,
        in_specs=placed,
        out_specs=(
            P(None, "row", "beam"),
            P(None, "beam", "row", None, None),
            P(None, "beam", "row", None, None),
            P(None, "beam", None, None, "row"),
        ),
        check_vma=False,
    )
```

```python
import jax
import jax.numpy as jnp
from jax import lax
from jax.experimental import pallas as pl
from jax.experimental.pallas import tpu as pltpu
from jax.sharding import PartitionSpec as P

EPS = 1e-05
F32 = jnp.float32
BF16 = jnp.bfloat16
STEPS = 4
SESS = 2
WIDTH = 16
BEAMS = SESS * WIDTH
ROWS = STEPS * BEAMS
HD = 64
NS = 256
GROUP_CH = 2048.0


def row_of(step, s, b):
    v = s * WIDTH + b
    return (v % 4) * 32 + (v // 4) * 4 + step


def dot(a, b):
    return jnp.dot(a, b, preferred_element_type=F32)


def dot_t(a, b):
    return lax.dot_general(a, b, (((1,), (1,)), ((), ())), preferred_element_type=F32)


def lineage(par):
    r = lax.broadcasted_iota(jnp.int32, (ROWS, 1), 0)
    t = r & 3
    s = (r & 31) >> 4
    before = (par & 3) * 32 + (s * 4 + (par >> 2)) * 4 + t - 1
    before = jnp.where(t > 0, before, -1)
    start = jnp.where(t == 0, (par >> 1) * 4 + s * 2 + (par & 1), -1)
    lanes = lax.broadcasted_iota(jnp.int32, (ROWS, ROWS), 1)
    a1 = jnp.where(lanes == before, 1.0, 0.0)
    lanes_i = lax.broadcasted_iota(jnp.int32, (ROWS, BEAMS), 1)
    g = jnp.where(lanes_i == start, 1.0, 0.0)
    a1b = a1.astype(BF16)
    a2 = dot(a1b, a1b)
    a3 = dot(a1b, a2.astype(BF16))
    gb = g.astype(BF16)
    g1 = dot(a1b, gb)
    g2 = dot(a1b, g1.astype(BF16))
    g3 = dot(a1b, g2.astype(BF16))
    return t, a1, a2, a3, g + g1 + g2 + g3


def head_part(ref, width):
    head = lax.axis_index("beam")
    part = jnp.zeros((ref.shape[0], width), F32)
    for h in range(8):
        part = part + jnp.where(head == h, ref[:, width * h : width * h + width].astype(F32), 0.0)
    return part


def head_value(ref):
    lane = lax.broadcasted_iota(jnp.int32, (1, 8), 1)
    return jnp.sum(jnp.where(lane == lax.axis_index("beam"), ref[...], 0.0), axis=1, keepdims=True)


def pack_kernel(state, *refs):
    outs, (held, sem_in, sem_out) = refs[:4], refs[4:]
    head = lax.axis_index("beam")
    loads = []
    for k in range(8):
        for j in range(4):
            loads.append(
                pltpu.make_async_copy(state.at[j // 2, j % 2, head ^ k], held.at[k // 2, k % 2, j], sem_in.at[k, j])
            )
            loads[-1].start()
    copies = []
    for c in range(4):
        for load in loads[8 * c : 8 * c + 8]:
            load.wait()
        copies.append(pltpu.make_async_copy(held.at[c], outs[c], sem_out.at[c]))
        copies[-1].start()
    for copy in copies:
        copy.wait()


def merge_kernel(p0, p1, p2, p3, out, sems):
    loads = [pltpu.make_async_copy(p.at[1], out.at[c], sems.at[c]) for c, p in enumerate((p0, p1, p2, p3))]
    for load in loads:
        load.start()
    for load in loads:
        load.wait()


def arrived(parts):
    return [(k, parts[4].at[k // 2] if k % 2 else parts[k // 2].at[0]) for k in range(8)]


def conv_kernel(recv, par, conv_x_w, conv_bc_w, sum_out, conv_out, bc_out, dt_out, fin_out, init):
    total = recv[0, 0:ROWS, :].astype(F32)
    dt = recv[0, 128:144, :].astype(F32)
    for k in range(3):
        init[k, 0:4, :] = dt[4 * k : 4 * k + 4]
    for i in range(1, 8):
        total = total + recv[i, 0:ROWS, :].astype(F32)
        extra = recv[i, 128:144, :].astype(F32)
        for k in range(3):
            init[k, 4 * i : 4 * i + 4, :] = extra[4 * k : 4 * k + 4]
        dt = dt + extra
    dt_out[...] = dt[12:13, 0:128] + dt[12:13, 128:256]
    new = total.astype(BF16)
    t, a1, a2, a3, g = lineage(par[...])
    gb = g.astype(BF16)
    start = [dot(gb, init[k].astype(BF16)) for k in range(3)]
    past1 = dot(a1.astype(BF16), new) + jnp.where(t == 0, start[2], 0.0)
    past2 = dot(a2.astype(BF16), new) + jnp.where(t == 0, start[1], 0.0) + jnp.where(t == 1, start[2], 0.0)
    past3 = (
        dot(a3.astype(BF16), new)
        + jnp.where(t == 0, start[0], 0.0)
        + jnp.where(t == 1, start[1], 0.0)
        + jnp.where(t == 2, start[2], 0.0)
    )
    w = jnp.concatenate([head_part(conv_x_w, HD), jnp.zeros((4, HD), F32), conv_bc_w[...].astype(F32)], axis=1)
    mixed = w[0:1] * past3 + w[1:2] * past2 + w[2:3] * past1 + w[3:4] * new.astype(F32)
    conv = mixed / (1.0 + jnp.exp(-mixed))
    sum_out[...] = new
    conv_out[...] = conv[:, 0:128].astype(BF16)
    bc_out[...] = conv[:, 128:256].astype(BF16)
    e = lax.broadcasted_iota(jnp.int32, (BEAMS, ROWS), 0)
    b = (e >> 2) * 2 + (e & 1)
    s = (e >> 1) & 1
    last = (b & 3) * 32 + (s * 4 + (b >> 2)) * 4 + STEPS - 1
    pick = jnp.where(lax.broadcasted_iota(jnp.int32, (BEAMS, ROWS), 1) == last, 1.0, 0.0).astype(BF16)
    fin_out[0] = dot(pick, past2.astype(BF16)).astype(BF16)
    fin_out[1] = dot(pick, past1.astype(BF16)).astype(BF16)
    fin_out[2] = dot(pick, new).astype(BF16)


def group_columns(blocks, low):
    b_cols, c_cols = [], []
    for q in range(4):
        part = jnp.zeros((ROWS, 128), F32)
        for k in range(4):
            part = part + jnp.where(low == (q ^ k), blocks[k], 0.0)
        b_cols.append(part[:, 0:64])
        c_cols.append(part[:, 64:128])
    return jnp.concatenate(b_cols, 1).astype(BF16), jnp.concatenate(c_cols, 1).astype(BF16)


def scan_kernel(
    par, new, conv, bc0, bc1, bc2, bc3, dt_raw, norm_gain, a_log, dt_bias, d_skip, *refs
):
    parts, (send_out, b_out, coef_out, first_out) = refs[:5], refs[5:9]
    state, send, b_buf, coef_buf, first_buf, sem_in, sem_send = refs[9:]
    head = lax.axis_index("beam")
    loads = [pltpu.make_async_copy(p, state.at[pl.ds((head ^ k) * 4, 4)], sem_in.at[k]) for k, p in arrived(parts)]
    for load in loads:
        load.start()
    low = lax.axis_index("row") & 3
    blocks = [ref[...].astype(F32) for ref in (bc0, bc1, bc2, bc3)]
    b_in, c_out = group_columns(blocks, low)
    t, a1, a2, a3, g = lineage(par[...])
    raw = dt_raw[...].astype(BF16).astype(F32) + head_value(dt_bias)
    step_size = jnp.maximum(raw, 0.0) + jnp.log1p(jnp.exp(-jnp.abs(raw)))
    rate = jnp.exp(head_value(a_log))
    log_decay = -rate * step_size
    rr = lax.broadcasted_iota(jnp.int32, (ROWS, ROWS), 0)
    cc = lax.broadcasted_iota(jnp.int32, (ROWS, ROWS), 1)
    eye = jnp.where(rr == cc, 1.0, 0.0)
    path1 = jnp.sum(eye * log_decay, axis=1, keepdims=True)
    path2 = path1 + jnp.sum(a1 * log_decay, axis=1, keepdims=True)
    path3 = path2 + jnp.sum(a2 * log_decay, axis=1, keepdims=True)
    path4 = path3 + jnp.sum(a3 * log_decay, axis=1, keepdims=True)
    coef = (eye + a1 * jnp.exp(path1) + a2 * jnp.exp(path2) + a3 * jnp.exp(path3)) * step_size
    first = jnp.exp(path4)
    x_conv = conv[:, 0:64]
    inner = dot_t(c_out, b_in) * coef
    read = jnp.dot(inner, x_conv.astype(F32), precision=lax.Precision.HIGHEST, preferred_element_type=F32)
    lanes_i = lax.broadcasted_iota(jnp.int32, (ROWS, BEAMS), 1).astype(F32)
    origin = jnp.sum(g * lanes_i, axis=1, keepdims=True)
    half = jnp.where(lax.broadcasted_iota(jnp.int32, (ROWS, 128), 1) < 64, 0.0, 1.0)
    origin_b = jnp.broadcast_to(origin, (ROWS, 128)) - half
    early = []
    b_buf[...] = b_in
    coef_buf[...] = coef
    first_buf[...] = jnp.broadcast_to(first, (ROWS, 128))
    for n, (buf, ref) in enumerate(((b_buf, b_out), (coef_buf, coef_out), (first_buf, first_out))):
        early.append(pltpu.make_async_copy(buf, ref, sem_send.at[8 + n]))
        early[-1].start()
    acc = jnp.zeros((ROWS, 128), F32)
    for load in loads:
        load.wait()
    for p in range(BEAMS // 2):
        both = state[2 * p : 2 * p + 2].reshape(2 * HD, NS)
        acc = acc + jnp.where(origin_b == float(2 * p), dot_t(c_out, both), 0.0)
    old = acc[:, 0:64] + acc[:, 64:128]
    x_val = x_conv.astype(F32)
    read = read + first * old + head_value(d_skip) * x_val
    gate = new[:, 64:128].astype(F32)
    gated = read * (gate / (1.0 + jnp.exp(-gate)))
    square = jnp.sum(gated * gated, axis=1, keepdims=True)
    high = square.astype(BF16).astype(F32)
    rest = square - high
    lane = lax.broadcasted_iota(jnp.int32, (ROWS, 64), 1)
    stats = jnp.where(lane == 0, high, jnp.where(lane == 1, rest, 0.0))
    send[...] = jnp.concatenate([gated * head_part(norm_gain, HD), stats], axis=1).astype(BF16)
    sends = [pltpu.make_async_copy(send, send_out.at[k], sem_send.at[k]) for k in range(8)]
    for copy in sends:
        copy.start()
    sends = early + sends
    for copy in sends:
        copy.wait()


def final_kernel(parents, conv, b_in, coef_ref, first_ref, fin, *refs):
    parts, homes = refs[:5], refs[5:9]
    state, block, sem_in, sem_home = refs[9:]
    head = lax.axis_index("beam")
    loads = [pltpu.make_async_copy(p, state.at[pl.ds((head ^ k) * 4, 4)], sem_in.at[k]) for k, p in arrived(parts)]
    for load in loads:
        load.start()
    x_t = conv[...].astype(F32).T[0:HD]
    b = b_in[...]
    for load in loads:
        load.wait()
    saves = []
    for i in range(8):
        rows = [row_of(STEPS - 1, j // 2, 2 * i + j % 2) for j in range(4)]
        left = jnp.concatenate([x_t * coef_ref[row : row + 1, :] for row in rows], axis=0).astype(BF16)
        update = dot(left, b)
        for j in range(4):
            s, at = j // 2, 2 * i + j % 2
            for step in range(STEPS - 1, -1, -1):
                at = parents[step * BEAMS + s * WIDTH + at]
            origin = (at >> 1) * 4 + s * 2 + (at & 1)
            keep = jnp.broadcast_to(first_ref[rows[j] : rows[j] + 1, 0:1], (HD, NS))
            value = keep * state[origin].astype(F32) + update[HD * j : HD * j + HD]
            block[i, HD * j : HD * j + HD, :] = value.astype(BF16)
        taps = [fin[k, 4 * i : 4 * i + 4, 0:64].astype(F32) for k in range(3)]
        tail = jnp.concatenate(taps + [jnp.zeros((4, 64), F32)], axis=1)
        block[i, 4 * HD : 4 * HD + 16, :] = jnp.concatenate([tail, jnp.zeros((12, NS), F32)], axis=0).astype(BF16)
    for k in range(8):
        saves.append(pltpu.make_async_copy(block.at[head ^ k], homes[k // 2].at[k % 2], sem_home.at[k]))
        saves[-1].start()
    for copy in saves:
        copy.wait()


def unpack_kernel(*refs):
    parts, (ssm_out, conv_out), (held, sem_in, sem_out) = refs[:5], refs[5:7], refs[7:]
    head = lax.axis_index("beam")
    loads = [pltpu.make_async_copy(p, held.at[head ^ k], sem_in.at[k]) for k, p in arrived(parts)]
    for load in loads:
        load.start()
    copies = []
    for k in range(8):
        loads[k].wait()
        h = head ^ k
        for j in range(4):
            src = held.at[h, pl.ds(HD * j, HD)]
            copies.append(pltpu.make_async_copy(src, ssm_out.at[j // 2, j % 2, h], sem_out.at[k, j]))
            copies[-1].start()
    for h in range(8):
        tail = held[h, 4 * HD : 4 * HD + 16, :].astype(F32)
        for j in range(4):
            for k in range(3):
                conv_out[j // 2, j % 2, k, h : h + 1, :] = tail[j : j + 1, HD * k : HD * k + HD].astype(BF16)
    for copy in copies:
        copy.wait()


def out_kernel(recv, w_out, out):
    stats = recv[0, :, 64:128].astype(F32)
    for i in range(1, 8):
        stats = stats + recv[i, :, 64:128].astype(F32)
    square = stats[:, 0:1] + stats[:, 1:2]
    high = square.astype(BF16).astype(F32)
    rest = square - high
    lane = lax.broadcasted_iota(jnp.int32, (ROWS, 128), 1)
    tail = jnp.where(lane == 0, high, jnp.where(lane == 1, rest, 0.0))
    left = jnp.concatenate([recv[i, :, 0:64] for i in range(8)], axis=1)
    full = jnp.concatenate([dot(left, w_out[...]), tail], axis=1)
    for q in range(4):
        for m in range(8):
            out[4 * m + q] = full[32 * q + 4 * m : 32 * q + 4 * m + 4].astype(BF16)


def norm_kernel(recv, out):
    result = jnp.zeros((STEPS, 1024), F32)
    for g in range(8):
        total = recv[4 * g].astype(F32)
        for j in range(1, 4):
            total = total + recv[4 * g + j].astype(F32)
        square = total[:, 1024:1025] + total[:, 1025:1026]
        result = result + total[:, 0:1024] * lax.rsqrt(square * (1.0 / GROUP_CH) + EPS)
    out[...] = result.astype(BF16)


VM = pl.BlockSpec(memory_space=pltpu.VMEM)
SM = pl.BlockSpec(memory_space=pltpu.SMEM)
ANY = pl.BlockSpec(memory_space=pl.ANY)
FAR = pl.BlockSpec(memory_space=pltpu.HBM)


def call(kernel, name, specs, outs, scratch=(), mib=6, out_specs=None):
    def build(*args):
        far = [n for n, spec in enumerate(specs) if spec is FAR]
        count = len(specs)
        buffers = [pltpu.VMEM(args[n].shape, args[n].dtype) for n in far]
        sems = [pltpu.SemaphoreType.DMA((len(far),))] if far else []

        def body(*refs):
            ins = list(refs[:count])
            rest = refs[count : count + len(outs) + len(scratch)]
            held = refs[count + len(outs) + len(scratch) :]
            copies = [pltpu.make_async_copy(ins[n], held[k], held[-1].at[k]) for k, n in enumerate(far)]
            for copy in copies:
                copy.start()
            for copy in copies:
                copy.wait()
            for k, n in enumerate(far):
                ins[n] = held[k]
            kernel(*ins, *rest)

        args = [
            pltpu.with_memory_space_constraint(arg, pltpu.HBM) if specs[n] in (ANY, FAR) else arg
            for n, arg in enumerate(args)
        ]
        return pl.pallas_call(
            body,
            name=name,
            in_specs=list(specs),
            out_specs=tuple(out_specs or [VM for _ in outs]),
            out_shape=tuple(
                pltpu.HBM(s, d) if out_specs and out_specs[n] is ANY else jax.ShapeDtypeStruct(s, d)
                for n, (s, d) in enumerate(outs)
            ),
            scratch_shapes=list(scratch) + buffers + sems,
            compiler_params=pltpu.CompilerParams(vmem_limit_bytes=mib << 20),
        )(*args)

    return build


def swap(value, axis, count, mask):
    return lax.ppermute(value, axis, [(i, i ^ mask) for i in range(count)])


def chips(blocks):
    return [blocks[0]] + [swap(blocks[c], "beam", 8, 2 * c) for c in range(1, 4)]


def cores(got, name):
    shape = (4,) + got[0].shape[1:]
    (merged,) = call(
        merge_kernel,
        name,
        [ANY] * 4,
        [(shape, BF16)],
        [pltpu.SemaphoreType.DMA((4,))],
    )(*got)
    return got + [swap(merged, "beam", 8, 1)]


def local(
    x_in,
    w_inner,
    w_bc,
    w_dt,
    conv_x_w,
    conv_bc_w,
    dt_bias,
    a_log,
    d_skip,
    norm_gain,
    w_out,
    ssm_state,
    conv_x_state,
    conv_bc_state,
    parents,
):
    beam = lax.axis_index("beam")
    d_local = x_in.shape[-1]
    heads = ssm_state.shape[2]
    parent_column = parents.reshape(STEPS, 8, 4).transpose(2, 1, 0).reshape(ROWS, 1)
    x = x_in.reshape(STEPS, 8, 4, d_local).transpose(2, 1, 0, 3).reshape(ROWS, d_local)

    inner = jnp.einsum("rd,dzk->rzk", x, w_inner, preferred_element_type=F32).astype(BF16)
    inner = inner[:, ::-1].reshape(ROWS, 2, heads, HD).transpose(2, 0, 1, 3).reshape(heads, ROWS, 2 * HD)
    bc = jnp.einsum("rd,dzk->rzk", x, w_bc, preferred_element_type=F32).astype(BF16).reshape(ROWS, 128)
    top = jnp.concatenate([inner, jnp.broadcast_to(bc[None], (heads, ROWS, 128))], axis=2)
    dt = jnp.einsum("dh,rd->hr", w_dt, x, preferred_element_type=F32)
    dt_high = lax.reduce_precision(dt, 8, 7)
    dt_row = jnp.concatenate([dt_high, dt - dt_high], axis=1).astype(BF16)[:, None]
    taps_x = conv_x_state.transpose(2, 4, 0, 1, 3).reshape(heads, 12, HD)
    taps_bc = jnp.broadcast_to(conv_bc_state.transpose(2, 0, 1, 3, 4).reshape(1, 12, 128), (heads, 12, 128))
    extra = jnp.concatenate([taps_x, jnp.zeros((heads, 12, HD), BF16), taps_bc], axis=2)
    bottom = jnp.concatenate([extra, dt_row, jnp.zeros((heads, 3, 256), BF16)], axis=1)
    payload = jnp.concatenate([top, bottom], axis=1)
    recv = lax.all_to_all(payload, "beam", split_axis=0, concat_axis=0, tiled=True)

    packed = call(
        pack_kernel,
        "pack",
        [ANY],
        [((2, 4, HD, NS), BF16)] * 4,
        [
            pltpu.VMEM((4, 2, 4, HD, NS), BF16),
            pltpu.SemaphoreType.DMA((8, 4)),
            pltpu.SemaphoreType.DMA((4,)),
        ],
        out_specs=[ANY] * 4,
    )(ssm_state)
    halves = chips(packed)

    new, conv, bc_conv, dt_raw, fin = call(
        conv_kernel,
        "conv",
        [VM, VM, VM, VM],
        [((ROWS, 256), BF16), ((ROWS, 128), BF16), ((ROWS, 128), BF16), ((1, ROWS), F32), ((3, BEAMS, 256), BF16)],
        [pltpu.VMEM((3, BEAMS, 256), F32)],
    )(recv, parent_column, conv_x_w, conv_bc_w.reshape(4, 128))

    others = [swap(bc_conv, "row", 32, k) for k in (1, 2, 3)]
    gated = lax.optimization_barrier((*others, *halves))
    others, halves = list(gated[:3]), list(gated[3:])
    states = cores(halves, "states")

    send, b_in, coef, first = call(
        scan_kernel,
        "scan",
        [VM] * 12 + [ANY] * 5,
        [((8, ROWS, 128), BF16), ((ROWS, NS), BF16), ((ROWS, ROWS), F32), ((ROWS, 128), F32)],
        [
            pltpu.VMEM((BEAMS, HD, NS), BF16),
            pltpu.VMEM((ROWS, 128), BF16),
            pltpu.VMEM((ROWS, NS), BF16),
            pltpu.VMEM((ROWS, ROWS), F32),
            pltpu.VMEM((ROWS, 128), F32),
            pltpu.SemaphoreType.DMA((8,)),
            pltpu.SemaphoreType.DMA((11,)),
        ],
        out_specs=[ANY] * 4,
    )(
        parent_column,
        new,
        conv,
        bc_conv,
        *others,
        dt_raw,
        norm_gain.reshape(1, 512),
        a_log.reshape(1, 8),
        dt_bias.reshape(1, 8),
        d_skip.reshape(1, 8),
        *states,
    )
    gathered = lax.all_to_all(send, "beam", split_axis=0, concat_axis=0, tiled=True)
    final = list(call(
        final_kernel,
        "final",
        [SM, VM] + [FAR] * 4 + [ANY] * 5,
        [((2, 4 * HD + 16, NS), BF16)] * 4,
        [
            pltpu.VMEM((BEAMS, HD, NS), BF16),
            pltpu.VMEM((8, 4 * HD + 16, NS), BF16),
            pltpu.SemaphoreType.DMA((8,)),
            pltpu.SemaphoreType.DMA((8,)),
        ],
        out_specs=[ANY] * 4,
    )(parents.reshape(ROWS), conv, b_in, coef, first, fin, *states))
    gathered, *final = lax.optimization_barrier((gathered, *final))
    homes = cores(chips(final), "finals")
    (parts,) = call(
        out_kernel,
        "project",
        [VM, VM],
        [((BEAMS, STEPS, 1152), BF16)],
    )(gathered, w_out)
    spread = lax.all_to_all(parts, "row", split_axis=0, concat_axis=0, tiled=True)
    ssm_final, conv_x_rows = call(
        unpack_kernel,
        "unpack",
        [ANY] * 5,
        [((SESS, 2, heads, HD, NS), BF16), ((SESS, 2, 3, heads, HD), BF16)],
        [
            pltpu.VMEM((8, 4 * HD + 16, NS), BF16),
            pltpu.SemaphoreType.DMA((8,)),
            pltpu.SemaphoreType.DMA((8, 4)),
        ],
        out_specs=[ANY, VM],
    )(*homes)
    spread, conv_x_rows = lax.optimization_barrier((spread, conv_x_rows))
    (layer_out,) = call(norm_kernel, "norm", [VM], [((STEPS, 1024), BF16)])(spread)
    layer_out = layer_out[:, None]
    conv_x_final = conv_x_rows.transpose(0, 1, 3, 4, 2)

    own = lax.dynamic_slice_in_dim(fin, beam * 4, 4, 1)[:, :, 128:]
    conv_bc_final = own.reshape(3, SESS, 2, 2, 64).transpose(1, 2, 0, 3, 4)
    return layer_out, ssm_final, conv_x_final, conv_bc_final


def solution(mesh):
    placed = (
        P(None, None, None, "beam"),
        P("beam", None, "row"),
        P("beam", None, "row"),
        P("beam", "row"),
        P(None, "row"),
        P(None, None, "row"),
        P("row"),
        P("row"),
        P("row"),
        P("row"),
        P("row", "beam"),
        P(None, "beam", "row", None, None),
        P(None, "beam", "row", None, None),
        P(None, "beam", None, None, "row"),
        P(),
    )
    return jax.shard_map(
        local,
        mesh=mesh,
        in_specs=placed,
        out_specs=(
            P(None, "row", "beam"),
            P(None, "beam", "row", None, None),
            P(None, "beam", "row", None, None),
            P(None, "beam", None, None, "row"),
        ),
        check_vma=False,
    )
```

```python
import jax
import jax.numpy as jnp
from jax import lax
from jax.experimental import pallas as pl
from jax.experimental.pallas import tpu as pltpu
from jax.sharding import PartitionSpec as P

EPS = 1e-05
F32 = jnp.float32
BF16 = jnp.bfloat16
STEPS = 4
SESS = 2
WIDTH = 16
BEAMS = SESS * WIDTH
ROWS = STEPS * BEAMS
HD = 64
NS = 256
GROUP_CH = 2048.0


def row_of(step, s, b):
    v = s * WIDTH + b
    return (v % 4) * 32 + (v // 4) * 4 + step


def dot(a, b):
    return jnp.dot(a, b, preferred_element_type=F32)


def dot_t(a, b):
    return lax.dot_general(a, b, (((1,), (1,)), ((), ())), preferred_element_type=F32)


def lineage(par):
    r = lax.broadcasted_iota(jnp.int32, (ROWS, 1), 0)
    t = r & 3
    s = (r & 31) >> 4
    before = (par & 3) * 32 + (s * 4 + (par >> 2)) * 4 + t - 1
    before = jnp.where(t > 0, before, -1)
    start = jnp.where(t == 0, (par >> 1) * 4 + s * 2 + (par & 1), -1)
    lanes = lax.broadcasted_iota(jnp.int32, (ROWS, ROWS), 1)
    a1 = jnp.where(lanes == before, 1.0, 0.0)
    lanes_i = lax.broadcasted_iota(jnp.int32, (ROWS, BEAMS), 1)
    g = jnp.where(lanes_i == start, 1.0, 0.0)
    a1b = a1.astype(BF16)
    a2 = dot(a1b, a1b)
    a3 = dot(a1b, a2.astype(BF16))
    gb = g.astype(BF16)
    g1 = dot(a1b, gb)
    g2 = dot(a1b, g1.astype(BF16))
    g3 = dot(a1b, g2.astype(BF16))
    return t, a1, a2, a3, g + g1 + g2 + g3


def head_part(ref, width):
    head = lax.axis_index("beam")
    part = jnp.zeros((ref.shape[0], width), F32)
    for h in range(8):
        part = part + jnp.where(head == h, ref[:, width * h : width * h + width].astype(F32), 0.0)
    return part


def head_value(ref):
    lane = lax.broadcasted_iota(jnp.int32, (1, 8), 1)
    return jnp.sum(jnp.where(lane == lax.axis_index("beam"), ref[...], 0.0), axis=1, keepdims=True)


def pack_kernel(state, *refs):
    outs, (held, sem_in, sem_out) = refs[:4], refs[4:]
    head = lax.axis_index("beam")
    loads = []
    for k in range(8):
        for j in range(4):
            loads.append(
                pltpu.make_async_copy(state.at[j // 2, j % 2, head ^ k], held.at[k // 2, k % 2, j], sem_in.at[k, j])
            )
            loads[-1].start()
    copies = []
    for c in range(4):
        for load in loads[8 * c : 8 * c + 8]:
            load.wait()
        copies.append(pltpu.make_async_copy(held.at[c], outs[c], sem_out.at[c]))
        copies[-1].start()
    for copy in copies:
        copy.wait()


def merge_kernel(p0, p1, p2, p3, out, sems):
    loads = [pltpu.make_async_copy(p.at[1], out.at[c], sems.at[c]) for c, p in enumerate((p0, p1, p2, p3))]
    for load in loads:
        load.start()
    for load in loads:
        load.wait()


def arrived(parts):
    return [(k, parts[4].at[k // 2] if k % 2 else parts[k // 2].at[0]) for k in range(8)]


def conv_kernel(recv, par, conv_x_w, conv_bc_w, sum_out, conv_out, bc_out, dt_out, fin_out, init):
    total = recv[0, 0:ROWS, :].astype(F32)
    dt = recv[0, 128:144, :].astype(F32)
    for k in range(3):
        init[k, 0:4, :] = dt[4 * k : 4 * k + 4]
    for i in range(1, 8):
        total = total + recv[i, 0:ROWS, :].astype(F32)
        extra = recv[i, 128:144, :].astype(F32)
        for k in range(3):
            init[k, 4 * i : 4 * i + 4, :] = extra[4 * k : 4 * k + 4]
        dt = dt + extra
    dt_out[...] = dt[12:13, 0:128] + dt[12:13, 128:256]
    new = total.astype(BF16)
    t, a1, a2, a3, g = lineage(par[...])
    gb = g.astype(BF16)
    start = [dot(gb, init[k].astype(BF16)) for k in range(3)]
    past1 = dot(a1.astype(BF16), new) + jnp.where(t == 0, start[2], 0.0)
    past2 = dot(a2.astype(BF16), new) + jnp.where(t == 0, start[1], 0.0) + jnp.where(t == 1, start[2], 0.0)
    past3 = (
        dot(a3.astype(BF16), new)
        + jnp.where(t == 0, start[0], 0.0)
        + jnp.where(t == 1, start[1], 0.0)
        + jnp.where(t == 2, start[2], 0.0)
    )
    w = jnp.concatenate([head_part(conv_x_w, HD), jnp.zeros((4, HD), F32), conv_bc_w[...].astype(F32)], axis=1)
    mixed = w[0:1] * past3 + w[1:2] * past2 + w[2:3] * past1 + w[3:4] * new.astype(F32)
    conv = mixed / (1.0 + jnp.exp(-mixed))
    sum_out[...] = new
    conv_out[...] = conv[:, 0:128].astype(BF16)
    bc_out[...] = conv[:, 128:256].astype(BF16)
    e = lax.broadcasted_iota(jnp.int32, (BEAMS, ROWS), 0)
    b = (e >> 2) * 2 + (e & 1)
    s = (e >> 1) & 1
    last = (b & 3) * 32 + (s * 4 + (b >> 2)) * 4 + STEPS - 1
    pick = jnp.where(lax.broadcasted_iota(jnp.int32, (BEAMS, ROWS), 1) == last, 1.0, 0.0).astype(BF16)
    fin_out[0] = dot(pick, past2.astype(BF16)).astype(BF16)
    fin_out[1] = dot(pick, past1.astype(BF16)).astype(BF16)
    fin_out[2] = dot(pick, new).astype(BF16)


def group_columns(blocks, low):
    b_cols, c_cols = [], []
    for q in range(4):
        part = jnp.zeros((ROWS, 128), F32)
        for k in range(4):
            part = part + jnp.where(low == (q ^ k), blocks[k], 0.0)
        b_cols.append(part[:, 0:64])
        c_cols.append(part[:, 64:128])
    return jnp.concatenate(b_cols, 1).astype(BF16), jnp.concatenate(c_cols, 1).astype(BF16)


def scan_kernel(
    par, new, conv, bc0, bc1, bc2, bc3, dt_raw, norm_gain, a_log, dt_bias, d_skip, *refs
):
    parts, (send_out, b_out, coef_out, first_out) = refs[:5], refs[5:9]
    state, send, b_buf, coef_buf, first_buf, sem_in, sem_send = refs[9:]
    head = lax.axis_index("beam")
    loads = [pltpu.make_async_copy(p, state.at[pl.ds((head ^ k) * 4, 4)], sem_in.at[k]) for k, p in arrived(parts)]
    for load in loads:
        load.start()
    low = lax.axis_index("row") & 3
    blocks = [ref[...].astype(F32) for ref in (bc0, bc1, bc2, bc3)]
    b_in, c_out = group_columns(blocks, low)
    t, a1, a2, a3, g = lineage(par[...])
    raw = dt_raw[...].astype(BF16).astype(F32) + head_value(dt_bias)
    step_size = jnp.maximum(raw, 0.0) + jnp.log1p(jnp.exp(-jnp.abs(raw)))
    rate = jnp.exp(head_value(a_log))
    log_decay = -rate * step_size
    rr = lax.broadcasted_iota(jnp.int32, (ROWS, ROWS), 0)
    cc = lax.broadcasted_iota(jnp.int32, (ROWS, ROWS), 1)
    eye = jnp.where(rr == cc, 1.0, 0.0)
    path1 = jnp.sum(eye * log_decay, axis=1, keepdims=True)
    path2 = path1 + jnp.sum(a1 * log_decay, axis=1, keepdims=True)
    path3 = path2 + jnp.sum(a2 * log_decay, axis=1, keepdims=True)
    path4 = path3 + jnp.sum(a3 * log_decay, axis=1, keepdims=True)
    coef = (eye + a1 * jnp.exp(path1) + a2 * jnp.exp(path2) + a3 * jnp.exp(path3)) * step_size
    first = jnp.exp(path4)
    x_conv = conv[:, 0:64]
    inner = dot_t(c_out, b_in) * coef
    read = jnp.dot(inner, x_conv.astype(F32), precision=lax.Precision.HIGHEST, preferred_element_type=F32)
    lanes_i = lax.broadcasted_iota(jnp.int32, (ROWS, BEAMS), 1).astype(F32)
    origin = jnp.sum(g * lanes_i, axis=1, keepdims=True)
    half = jnp.where(lax.broadcasted_iota(jnp.int32, (ROWS, 128), 1) < 64, 0.0, 1.0)
    origin_b = jnp.broadcast_to(origin, (ROWS, 128)) - half
    early = []
    b_buf[...] = b_in
    coef_buf[...] = coef
    first_buf[...] = jnp.broadcast_to(first, (ROWS, 128))
    for n, (buf, ref) in enumerate(((b_buf, b_out), (coef_buf, coef_out), (first_buf, first_out))):
        early.append(pltpu.make_async_copy(buf, ref, sem_send.at[8 + n]))
        early[-1].start()
    acc = jnp.zeros((ROWS, 128), F32)
    for load in loads:
        load.wait()
    for p in range(BEAMS // 2):
        both = state[2 * p : 2 * p + 2].reshape(2 * HD, NS)
        acc = acc + jnp.where(origin_b == float(2 * p), dot_t(c_out, both), 0.0)
    old = acc[:, 0:64] + acc[:, 64:128]
    x_val = x_conv.astype(F32)
    read = read + first * old + head_value(d_skip) * x_val
    gate = new[:, 64:128].astype(F32)
    gated = read * (gate / (1.0 + jnp.exp(-gate)))
    square = jnp.sum(gated * gated, axis=1, keepdims=True)
    high = square.astype(BF16).astype(F32)
    rest = square - high
    lane = lax.broadcasted_iota(jnp.int32, (ROWS, 64), 1)
    stats = jnp.where(lane == 0, high, jnp.where(lane == 1, rest, 0.0))
    send[...] = jnp.concatenate([gated * head_part(norm_gain, HD), stats], axis=1).astype(BF16)
    sends = [pltpu.make_async_copy(send, send_out.at[k], sem_send.at[k]) for k in range(8)]
    for copy in sends:
        copy.start()
    sends = early + sends
    for copy in sends:
        copy.wait()


def final_kernel(parents, conv, b_in, coef_ref, first_ref, fin, *refs):
    parts, homes = refs[:5], refs[5:9]
    state, block, sem_in, sem_home = refs[9:]
    head = lax.axis_index("beam")
    loads = [pltpu.make_async_copy(p, state.at[pl.ds((head ^ k) * 4, 4)], sem_in.at[k]) for k, p in arrived(parts)]
    for load in loads:
        load.start()
    x_t = conv[...].astype(F32).T[0:HD]
    b = b_in[...]
    for load in loads:
        load.wait()
    saves = []
    for i in range(8):
        rows = [row_of(STEPS - 1, j // 2, 2 * i + j % 2) for j in range(4)]
        left = jnp.concatenate([x_t * coef_ref[row : row + 1, :] for row in rows], axis=0).astype(BF16)
        update = dot(left, b)
        for j in range(4):
            s, at = j // 2, 2 * i + j % 2
            for step in range(STEPS - 1, -1, -1):
                at = parents[step * BEAMS + s * WIDTH + at]
            origin = (at >> 1) * 4 + s * 2 + (at & 1)
            keep = jnp.broadcast_to(first_ref[rows[j] : rows[j] + 1, 0:1], (HD, NS))
            value = keep * state[origin].astype(F32) + update[HD * j : HD * j + HD]
            block[i, HD * j : HD * j + HD, :] = value.astype(BF16)
        taps = [fin[k, 4 * i : 4 * i + 4, 0:64].astype(F32) for k in range(3)]
        tail = jnp.concatenate(taps + [jnp.zeros((4, 64), F32)], axis=1)
        block[i, 4 * HD : 4 * HD + 16, :] = jnp.concatenate([tail, jnp.zeros((12, NS), F32)], axis=0).astype(BF16)
    for k in range(8):
        saves.append(pltpu.make_async_copy(block.at[head ^ k], homes[k // 2].at[k % 2], sem_home.at[k]))
        saves[-1].start()
    for copy in saves:
        copy.wait()


def unpack_kernel(*refs):
    parts, (ssm_out, conv_out), (held, sem_in, sem_out) = refs[:5], refs[5:7], refs[7:]
    head = lax.axis_index("beam")
    loads = [pltpu.make_async_copy(p, held.at[head ^ k], sem_in.at[k]) for k, p in arrived(parts)]
    for load in loads:
        load.start()
    copies = []
    for k in range(8):
        loads[k].wait()
        h = head ^ k
        for j in range(4):
            src = held.at[h, pl.ds(HD * j, HD)]
            copies.append(pltpu.make_async_copy(src, ssm_out.at[j // 2, j % 2, h], sem_out.at[k, j]))
            copies[-1].start()
    for h in range(8):
        tail = held[h, 4 * HD : 4 * HD + 16, :].astype(F32)
        for j in range(4):
            for k in range(3):
                conv_out[j // 2, j % 2, k, h : h + 1, :] = tail[j : j + 1, HD * k : HD * k + HD].astype(BF16)
    for copy in copies:
        copy.wait()


def out_kernel(recv, w_out, out):
    stats = recv[0, :, 64:128].astype(F32)
    for i in range(1, 8):
        stats = stats + recv[i, :, 64:128].astype(F32)
    square = stats[:, 0:1] + stats[:, 1:2]
    high = square.astype(BF16).astype(F32)
    rest = square - high
    lane = lax.broadcasted_iota(jnp.int32, (ROWS, 128), 1)
    tail = jnp.where(lane == 0, high, jnp.where(lane == 1, rest, 0.0))
    left = jnp.concatenate([recv[i, :, 0:64] for i in range(8)], axis=1)
    full = jnp.concatenate([dot(left, w_out[...]), tail], axis=1)
    for q in range(4):
        for m in range(8):
            out[4 * m + q] = full[32 * q + 4 * m : 32 * q + 4 * m + 4].astype(BF16)


def norm_kernel(recv, out):
    result = jnp.zeros((STEPS, 1024), F32)
    for g in range(8):
        total = recv[4 * g].astype(F32)
        for j in range(1, 4):
            total = total + recv[4 * g + j].astype(F32)
        square = total[:, 1024:1025] + total[:, 1025:1026]
        result = result + total[:, 0:1024] * lax.rsqrt(square * (1.0 / GROUP_CH) + EPS)
    out[...] = result.astype(BF16)


VM = pl.BlockSpec(memory_space=pltpu.VMEM)
SM = pl.BlockSpec(memory_space=pltpu.SMEM)
ANY = pl.BlockSpec(memory_space=pl.ANY)
FAR = pl.BlockSpec(memory_space=pltpu.HBM)


def call(kernel, name, specs, outs, scratch=(), mib=6, out_specs=None):
    def build(*args):
        far = [n for n, spec in enumerate(specs) if spec is FAR]
        count = len(specs)
        buffers = [pltpu.VMEM(args[n].shape, args[n].dtype) for n in far]
        sems = [pltpu.SemaphoreType.DMA((len(far),))] if far else []

        def body(*refs):
            ins = list(refs[:count])
            rest = refs[count : count + len(outs) + len(scratch)]
            held = refs[count + len(outs) + len(scratch) :]
            copies = [pltpu.make_async_copy(ins[n], held[k], held[-1].at[k]) for k, n in enumerate(far)]
            for copy in copies:
                copy.start()
            for copy in copies:
                copy.wait()
            for k, n in enumerate(far):
                ins[n] = held[k]
            kernel(*ins, *rest)

        args = [
            pltpu.with_memory_space_constraint(arg, pltpu.HBM) if specs[n] in (ANY, FAR) else arg
            for n, arg in enumerate(args)
        ]
        return pl.pallas_call(
            body,
            name=name,
            in_specs=list(specs),
            out_specs=tuple(out_specs or [VM for _ in outs]),
            out_shape=tuple(
                pltpu.HBM(s, d) if out_specs and out_specs[n] is ANY else jax.ShapeDtypeStruct(s, d)
                for n, (s, d) in enumerate(outs)
            ),
            scratch_shapes=list(scratch) + buffers + sems,
            compiler_params=pltpu.CompilerParams(vmem_limit_bytes=mib << 20),
        )(*args)

    return build


def swap(value, axis, count, mask):
    return lax.ppermute(value, axis, [(i, i ^ mask) for i in range(count)])


def chips(blocks):
    return [blocks[0]] + [swap(blocks[c], "beam", 8, 2 * c) for c in range(1, 4)]


def cores(got, name):
    shape = (4,) + got[0].shape[1:]
    (merged,) = call(
        merge_kernel,
        name,
        [ANY] * 4,
        [(shape, BF16)],
        [pltpu.SemaphoreType.DMA((4,))],
    )(*got)
    return got + [swap(merged, "beam", 8, 1)]


def local(
    x_in,
    w_inner,
    w_bc,
    w_dt,
    conv_x_w,
    conv_bc_w,
    dt_bias,
    a_log,
    d_skip,
    norm_gain,
    w_out,
    ssm_state,
    conv_x_state,
    conv_bc_state,
    parents,
):
    beam = lax.axis_index("beam")
    d_local = x_in.shape[-1]
    heads = ssm_state.shape[2]
    parent_column = parents.reshape(STEPS, 8, 4).transpose(2, 1, 0).reshape(ROWS, 1)
    x = x_in.reshape(STEPS, 8, 4, d_local).transpose(2, 1, 0, 3).reshape(ROWS, d_local)

    inner = jnp.einsum("rd,dzk->rzk", x, w_inner, preferred_element_type=F32).astype(BF16)
    inner = inner[:, ::-1].reshape(ROWS, 2, heads, HD).transpose(2, 0, 1, 3).reshape(heads, ROWS, 2 * HD)
    bc = jnp.einsum("rd,dzk->rzk", x, w_bc, preferred_element_type=F32).astype(BF16).reshape(ROWS, 128)
    top = jnp.concatenate([inner, jnp.broadcast_to(bc[None], (heads, ROWS, 128))], axis=2)
    dt = jnp.einsum("dh,rd->hr", w_dt, x, preferred_element_type=F32)
    dt_high = lax.reduce_precision(dt, 8, 7)
    dt_row = jnp.concatenate([dt_high, dt - dt_high], axis=1).astype(BF16)[:, None]
    taps_x = conv_x_state.transpose(2, 4, 0, 1, 3).reshape(heads, 12, HD)
    taps_bc = jnp.broadcast_to(conv_bc_state.transpose(2, 0, 1, 3, 4).reshape(1, 12, 128), (heads, 12, 128))
    extra = jnp.concatenate([taps_x, jnp.zeros((heads, 12, HD), BF16), taps_bc], axis=2)
    bottom = jnp.concatenate([extra, dt_row, jnp.zeros((heads, 3, 256), BF16)], axis=1)
    payload = jnp.concatenate([top, bottom], axis=1)
    recv = lax.all_to_all(payload, "beam", split_axis=0, concat_axis=0, tiled=True)

    packed = call(
        pack_kernel,
        "pack",
        [ANY],
        [((2, 4, HD, NS), BF16)] * 4,
        [
            pltpu.VMEM((4, 2, 4, HD, NS), BF16),
            pltpu.SemaphoreType.DMA((8, 4)),
            pltpu.SemaphoreType.DMA((4,)),
        ],
        out_specs=[ANY] * 4,
    )(ssm_state)
    halves = chips(packed)

    new, conv, bc_conv, dt_raw, fin = call(
        conv_kernel,
        "conv",
        [VM, VM, VM, VM],
        [((ROWS, 256), BF16), ((ROWS, 128), BF16), ((ROWS, 128), BF16), ((1, ROWS), F32), ((3, BEAMS, 256), BF16)],
        [pltpu.VMEM((3, BEAMS, 256), F32)],
    )(recv, parent_column, conv_x_w, conv_bc_w.reshape(4, 128))

    others = [swap(bc_conv, "row", 32, k) for k in (1, 2, 3)]
    gated = lax.optimization_barrier((*others, *halves))
    others, halves = list(gated[:3]), list(gated[3:])
    states = cores(halves, "states")

    send, b_in, coef, first = call(
        scan_kernel,
        "scan",
        [VM] * 12 + [ANY] * 4 + [VM],
        [((8, ROWS, 128), BF16), ((ROWS, NS), BF16), ((ROWS, ROWS), F32), ((ROWS, 128), F32)],
        [
            pltpu.VMEM((BEAMS, HD, NS), BF16),
            pltpu.VMEM((ROWS, 128), BF16),
            pltpu.VMEM((ROWS, NS), BF16),
            pltpu.VMEM((ROWS, ROWS), F32),
            pltpu.VMEM((ROWS, 128), F32),
            pltpu.SemaphoreType.DMA((8,)),
            pltpu.SemaphoreType.DMA((11,)),
        ],
        out_specs=[ANY] * 4,
    )(
        parent_column,
        new,
        conv,
        bc_conv,
        *others,
        dt_raw,
        norm_gain.reshape(1, 512),
        a_log.reshape(1, 8),
        dt_bias.reshape(1, 8),
        d_skip.reshape(1, 8),
        *states,
    )
    gathered = lax.all_to_all(send, "beam", split_axis=0, concat_axis=0, tiled=True)
    final = list(call(
        final_kernel,
        "final",
        [SM, VM] + [FAR] * 4 + [ANY] * 5,
        [((2, 4 * HD + 16, NS), BF16)] * 4,
        [
            pltpu.VMEM((BEAMS, HD, NS), BF16),
            pltpu.VMEM((8, 4 * HD + 16, NS), BF16),
            pltpu.SemaphoreType.DMA((8,)),
            pltpu.SemaphoreType.DMA((8,)),
        ],
        out_specs=[ANY] * 4,
    )(parents.reshape(ROWS), conv, b_in, coef, first, fin, *states))
    gathered, *final = lax.optimization_barrier((gathered, *final))
    homes = cores(chips(final), "finals")
    (parts,) = call(
        out_kernel,
        "project",
        [VM, VM],
        [((BEAMS, STEPS, 1152), BF16)],
    )(gathered, w_out)
    spread = lax.all_to_all(parts, "row", split_axis=0, concat_axis=0, tiled=True)
    ssm_final, conv_x_rows = call(
        unpack_kernel,
        "unpack",
        [ANY] * 5,
        [((SESS, 2, heads, HD, NS), BF16), ((SESS, 2, 3, heads, HD), BF16)],
        [
            pltpu.VMEM((8, 4 * HD + 16, NS), BF16),
            pltpu.SemaphoreType.DMA((8,)),
            pltpu.SemaphoreType.DMA((8, 4)),
        ],
        out_specs=[ANY, VM],
    )(*homes)
    spread, conv_x_rows = lax.optimization_barrier((spread, conv_x_rows))
    (layer_out,) = call(norm_kernel, "norm", [VM], [((STEPS, 1024), BF16)])(spread)
    layer_out = layer_out[:, None]
    conv_x_final = conv_x_rows.transpose(0, 1, 3, 4, 2)

    own = lax.dynamic_slice_in_dim(fin, beam * 4, 4, 1)[:, :, 128:]
    conv_bc_final = own.reshape(3, SESS, 2, 2, 64).transpose(1, 2, 0, 3, 4)
    return layer_out, ssm_final, conv_x_final, conv_bc_final


def solution(mesh):
    placed = (
        P(None, None, None, "beam"),
        P("beam", None, "row"),
        P("beam", None, "row"),
        P("beam", "row"),
        P(None, "row"),
        P(None, None, "row"),
        P("row"),
        P("row"),
        P("row"),
        P("row"),
        P("row", "beam"),
        P(None, "beam", "row", None, None),
        P(None, "beam", "row", None, None),
        P(None, "beam", None, None, "row"),
        P(),
    )
    return jax.shard_map(
        local,
        mesh=mesh,
        in_specs=placed,
        out_specs=(
            P(None, "row", "beam"),
            P(None, "beam", "row", None, None),
            P(None, "beam", "row", None, None),
            P(None, "beam", None, None, "row"),
        ),
        check_vma=False,
    )
```
